32 devices in a mesh: groups: 2 (over y), row: 8 (over z, x), col: 2 (over core).
Axes of the slice: x: 2, y: 2, z: 4, core: 2. Of those that a mesh axis runs over, the one named last changes fastest.
Arguments:
- features: bfloat16 [2048, 2048], P(('groups', 'row'), 'col'), parts along dimension 0, may hold values from -6 to 6
- tiles: bfloat16 [16, 8, 128, 128], P(('groups', 'row')), parts along dimension 0, may hold values from -6 to 6
- pattern: int32 [16, 8], P(('groups', 'row')), parts along dimension 0, may hold values from 0 to 7, as said below
- degrees: int32 [2048], P(('groups', 'row')), parts along dimension 0, may hold values from 16 to 63
- segments: int32 [2048], P(('groups', 'row')), parts along dimension 0, may hold values from 0 to 7, never falling along the last dimension, each value on 1 to 192 neighbouring positions
- pairs: int32 [128, 3], P('groups'), parts along dimension 0, may hold values from 0 to 15, as said below
- w_self: bfloat16 [128, 128], replicated, may hold values from -0.5 to 0.5
- w_neigh: bfloat16 [128, 128], replicated, may hold values from -0.5 to 0.5
- bias: float32 [128], replicated, may hold values from -3 to 3
- w_out: float32 [128], replicated, may hold values from -0.5 to 0.5
Outputs:
- loss: float32 [2], P('groups'), parts along dimension 0
- grad_self: float32 [256, 128], P('groups'), parts along dimension 0
- grad_neigh: float32 [256, 128], P('groups'), parts along dimension 0
- grad_bias: float32 [256], P('groups'), parts along dimension 0
- grad_out: float32 [256], P('groups'), parts along dimension 0
- node_grad: bfloat16 [2048, 2048], P(('groups', 'row'), 'col'), parts along dimension 0
The draws below stay inside these ranges and needn't reach their ends.
There are 2 independent parts, one for each index of `groups`. The reference program is written for one: setup_inputs(seed, part) draws one part's arguments, and reference() takes and returns one part's arrays. A program takes and returns all parts, laid end to end along the dimension named above; an argument that names none is the same for every part. Nothing has to cross between parts.
Inputs may be any that keep to these rules, and one draw needn't show every extreme that they name: `pattern`: block row i names only block columns held by the device that holds block row i or by the 2 devices before it along row, and its slot 0 names i itself. `pairs`: A pair's first entry is a segment, the other two are different configurations.
All inputs are finite; a program needn't handle non-finite values.
Results may differ from the reference program's by a relative error of at most 0.0059.
Values may be sent and summed in bfloat16 or wider, within the bound.
No kernel may reach another device: no remote copies, remote signals or barrier semaphores. Data moves between devices by JAX's collectives and lax.ppermute only.
A program may use at most 64 MiB of HBM per device.

```python
import math
import jax
import jax.numpy as jnp
import numpy as np
from jax import lax

HID = 128
TILE = 128
CONF = 16
K_TILES = 8
REACH = 2
SEGS = 8
PAIRS = 64
NB_DEV = 1
NODES = 1024


def draw_pattern(key, part):
    blocks = NODES // TILE
    block_row = jnp.arange(blocks, dtype=jnp.int32)
    device = block_row // NB_DEV
    key_back, key_pick = jax.random.split(jax.random.fold_in(key, 11))
    distance = jax.random.randint(key_back, (blocks, K_TILES), 0, REACH + 1)
    source = jnp.maximum(device[:, None] - distance, 0)
    column = source * NB_DEV + jax.random.randint(key_pick, (blocks, K_TILES), 0, NB_DEV)
    column = jnp.concatenate([block_row[:, None], column[:, 1:]], axis=1)
    return column.astype(jnp.int32)


def draw_pairs(key, part):
    key_seg, key_first, key_step = jax.random.split(jax.random.fold_in(key, 23), 3)
    index = jnp.arange(PAIRS, dtype=jnp.int32)
    segment = jax.random.randint(key_seg, (PAIRS,), 0, SEGS)
    segment = jnp.where(index == 0, SEGS - 1, segment)
    first = jax.random.randint(key_first, (PAIRS,), 0, CONF)
    first = jnp.where(index == 0, CONF - 1, first)
    second = (first + jax.random.randint(key_step, (PAIRS,), 1, CONF)) % CONF
    return jnp.stack([segment, first, second], axis=1).astype(jnp.int32)


def plant(values, stream_key, smallest, high):
    spot = [jax.random.randint(jax.random.fold_in(stream_key, axis), (), 0, length) for axis, length in enumerate(values.shape)]
    main_axis = values.shape.index(max(values.shape))
    next_to = spot[:main_axis] + [(spot[main_axis] + 1) % values.shape[main_axis]] + spot[main_axis + 1:]
    return values.at[tuple(spot)].set(smallest).at[tuple(next_to)].set(high)


def level_of(own_key, dims, cuts, smallest, top_value):
    def one(dim, parts):
        draws = jax.random.uniform(jax.random.fold_in(jax.random.fold_in(own_key, 6), dim), (parts,), jnp.float32, smallest / len(cuts), top_value / len(cuts))
        return jnp.repeat(jnp.exp(draws), dims[dim] // parts).reshape((-1,) + (1,) * (len(dims) - dim - 1))

    level = one(*cuts[0])
    for cut in cuts[1:]:
        level = level * one(*cut)
    return level


def length_profile(amount, total, reach, slope):
    loads = [(1 << 20) // math.isqrt(grade ** slope) + 1 for grade in range(2, amount + 1)]
    rest, given = total - reach - (amount - 1), [1] * (amount - 1)
    while rest > 0:
        candidates = [i for i in range(amount - 1) if given[i] < reach]
        whole, left = sum([loads[i] for i in candidates]), rest
        for i in candidates:
            more = min(reach - given[i], max(1, left * loads[i] // whole), rest)
            given[i] = given[i] + more
            rest = rest - more
    return np.array([reach] + given)


def uneven_parts(stream_key, amount, total, limit, lean):
    if amount == 2:
        one = jax.random.randint(stream_key, (), max(1, total - limit), min(limit, total - 1) + 1)
        return jnp.stack([one, total - one])
    lengths = jnp.asarray(length_profile(amount, total, limit, lean), jnp.int32)
    pairs = (amount - 1) // 2
    giver, receiver = lengths[1:1 + 2 * pairs:2], lengths[2:2 + 2 * pairs:2]
    slack = jnp.minimum(giver - 1, limit - receiver)
    shifted = jax.random.randint(jax.random.fold_in(stream_key, 1), (pairs,), 0, 1 << 20) % (slack + 1)
    lengths = lengths.at[1:1 + 2 * pairs:2].set(giver - shifted).at[2:2 + 2 * pairs:2].set(receiver + shifted)
    return lengths[jax.random.permutation(jax.random.fold_in(stream_key, 2), amount)]


def gaussian(own_key, dims, scale, bound, cuts=(), kind=jnp.bfloat16):
    loudness = level_of(own_key, dims, cuts, -0.22, 0.18) if cuts else 1.0
    drawn = jax.random.normal(own_key, dims, jnp.float32) * scale * loudness
    return jnp.minimum(jnp.maximum(drawn, -bound), bound).astype(kind)


def setup_inputs(seed: int = 0, part: int = 0) -> dict:
    keys = jax.random.split(jax.random.key(seed), 11)
    part_splits = jax.random.split(jax.random.fold_in(keys[10], part), 11)
    return {
        "features": gaussian(part_splits[0], (NODES, CONF * HID), 1.0, 6.0, ((0, 8), (1, 2))),
        "tiles": gaussian(part_splits[1], (NODES // TILE, K_TILES, TILE, TILE), 1.0, 6.0, ((0, 8),)),
        "pattern": draw_pattern(jax.random.fold_in(jax.random.fold_in(keys[10], part), 71), part),
        "degrees": plant(jax.random.randint(part_splits[3], (NODES,), max(1, K_TILES * TILE // 64), max(4, K_TILES * TILE // 16)), jax.random.fold_in(part_splits[3], 1), max(1, K_TILES * TILE // 64), (max(4, K_TILES * TILE // 16)) - 1).astype(jnp.int32),
        "segments": jnp.searchsorted(jnp.cumsum(uneven_parts(part_splits[4], SEGS, NODES, NODES // SEGS + NODES // (2 * SEGS), 2)), jnp.arange(NODES), side="right").astype(jnp.int32),
        "pairs": draw_pairs(jax.random.fold_in(jax.random.fold_in(keys[10], part), 71), part),
        "w_self": gaussian(keys[6], (HID, HID), HID ** -0.5, 0.5),
        "w_neigh": gaussian(keys[7], (HID, HID), HID ** -0.5, 0.5),
        "bias": gaussian(keys[8], (HID,), 0.5, 3.0, (), jnp.float32),
        "w_out": gaussian(keys[9], (HID,), HID ** -0.5, 0.5, (), jnp.float32),
    }


def silu_slope(value):
    sigm = jax.nn.sigmoid(value)
    return sigm * (1.0 + value * (1.0 - sigm))

def reference(features, tiles, pattern, degrees, segments, pairs, w_self, w_neigh, bias, w_out):
    blocks = NODES // TILE
    width = CONF * HID
    highest = lax.Precision.HIGHEST
    grid = features.reshape(blocks, TILE, width)
    summed = jnp.zeros((blocks, TILE, width), jnp.float32)
    for slot_index in range(K_TILES):
        panels = jnp.take(grid, pattern[:, slot_index], axis=0)
        summed = summed + jnp.einsum('brs,bsc->brc', tiles[:, slot_index].astype(jnp.float32), panels.astype(jnp.float32))
    degree = degrees.astype(jnp.float32)[:, None]
    mean_agg = (summed.reshape(NODES, width) / degree).astype(jnp.bfloat16)
    rows_x = features.reshape(NODES * CONF, HID)
    rows_a = mean_agg.reshape(NODES * CONF, HID)
    pre = jnp.dot(rows_x, w_self, preferred_element_type=jnp.float32) + jnp.dot(rows_a, w_neigh, preferred_element_type=jnp.float32) + bias
    hidden = jax.nn.silu(pre)
    node_score = jnp.einsum('ncd,d->nc', hidden.reshape(NODES, CONF, HID), w_out, precision=highest)
    member = (segments[:, None] == jnp.arange(SEGS, dtype=jnp.int32)[None, :]).astype(jnp.float32)
    seg_sums = jnp.dot(member.T, node_score, precision=highest, preferred_element_type=jnp.float32)
    counts = lax.optimization_barrier(jnp.sum(member, axis=0))
    root = jnp.sqrt(counts)
    scores = seg_sums / root[:, None]
    seg_hot = (pairs[:, 0:1] == jnp.arange(SEGS, dtype=jnp.int32)[None, :]).astype(jnp.float32)
    first_hot = (pairs[:, 1:2] == jnp.arange(CONF, dtype=jnp.int32)[None, :]).astype(jnp.float32)
    second_hot = (pairs[:, 2:3] == jnp.arange(CONF, dtype=jnp.int32)[None, :]).astype(jnp.float32)
    signed = first_hot - second_hot
    picked = jnp.dot(seg_hot, scores, precision=highest, preferred_element_type=jnp.float32)
    margin = jnp.maximum(0.0, 1.0 - lax.optimization_barrier(jnp.sum(picked * signed, axis=1)))
    loss = jnp.sum(margin * margin).reshape(1)
    d_scores = jnp.dot(seg_hot.T, (-2.0 * margin)[:, None] * signed, precision=highest, preferred_element_type=jnp.float32)
    d_node = jnp.dot(member, d_scores / root[:, None], precision=highest, preferred_element_type=jnp.float32)
    d_pre = d_node[:, :, None] * w_out * silu_slope(pre.reshape(NODES, CONF, HID))
    d_pre_b = d_pre.reshape(NODES * CONF, HID).astype(jnp.bfloat16)
    grad_self = jnp.dot(rows_x.T, d_pre_b, preferred_element_type=jnp.float32)
    grad_neigh = jnp.dot(rows_a.T, d_pre_b, preferred_element_type=jnp.float32)
    grad_bias = lax.optimization_barrier(jnp.sum(d_pre, axis=(0, 1)))
    grad_out = jnp.einsum('ncd,nc->d', hidden.reshape(NODES, CONF, HID), d_node, precision=highest)
    direct_term = jnp.dot(d_pre_b, w_self.T, preferred_element_type=jnp.float32).reshape(NODES, width)
    back = (jnp.dot(d_pre_b, w_neigh.T, preferred_element_type=jnp.float32).reshape(NODES, width) / degree).astype(jnp.bfloat16)
    back_blocks = back.reshape(blocks, TILE, width).astype(jnp.float32)
    spread = jnp.zeros((blocks, TILE, width), jnp.float32)
    for slot_index in range(K_TILES):
        contrib = jnp.einsum('brs,brc->bsc', tiles[:, slot_index].astype(jnp.float32), back_blocks)
        spread = spread + jax.ops.segment_sum(contrib, pattern[:, slot_index], num_segments=blocks)
    scale = math.sqrt(NODES / SEGS)
    node_grad = ((direct_term + spread.reshape(NODES, width)) * scale).astype(jnp.bfloat16)
    return (loss, grad_self, grad_neigh, grad_bias, grad_out, node_grad)
```

```python
import functools
import math

import jax
import jax.numpy as jnp
from jax import lax
from jax.experimental import pallas as pl
from jax.experimental.pallas import tpu as pltpu
from jax.sharding import PartitionSpec as P

REACH = 2
SEGS = 8
WINDOW = REACH + 1
F32 = jnp.float32
BF16 = jnp.bfloat16
HIGHEST = lax.Precision.HIGHEST
VMEM = pl.BlockSpec(memory_space=pltpu.VMEM)
SMEM = pl.BlockSpec(memory_space=pltpu.SMEM)
LIMIT = 24 << 20


def shifted(value, axis, steps):
    count = lax.axis_size(axis)
    initial, last = (max(0, -steps), min(count, count - steps))
    return lax.ppermute(value, axis, [(source, source + steps) for source in range(initial, last)])


def exchanged(value, axis, bit):
    count = lax.axis_size(axis)
    return lax.ppermute(value, axis, [(source, source ^ bit) for source in range(count)])


def mm(left, right, contract=((1,), (0,))):
    return lax.dot_general(left, right, (contract, ((), ())), preferred_element_type=F32)


def mm_exact(left, right, contract):
    return lax.dot_general(
        left, right, (contract, ((), ())), precision=HIGHEST, preferred_element_type=F32
    )


def split_two(value):
    high = value.astype(BF16)
    return high, (value - high.astype(F32)).astype(BF16)


def forward_kernel(
    local_confs,
    place_ref,
    ids_ref,
    own_ref,
    near_ref,
    far_ref,
    tiles_ref,
    degree_ref,
    segments_ref,
    w_self_ref,
    w_neigh_ref,
    bias_ref,
    w_out_ref,
    mean_ref,
    slope_ref,
    hidden_sum_ref,
    message_ref,
    tile_high_ref,
    tile_low_ref,
):
    hid = w_self_ref.shape[0]
    window = (far_ref, near_ref, own_ref)
    summed = None
    for reach in range(WINDOW):
        total = None
        for slot in range(tiles_ref.shape[1]):
            keep = (ids_ref[0, slot] == reach).astype(F32)
            term = tiles_ref[0, slot].astype(F32) * keep
            total = term if total is None else total + term
        high, low = split_two(total)
        tile_high_ref[reach] = high
        tile_low_ref[reach] = low
        panel = window[reach][...]
        term = mm(high, panel) + mm(low, panel)
        summed = term if summed is None else summed + term
    inverse = 1.0 / degree_ref[...]
    w_out = w_out_ref[...]
    seg_iota = lax.broadcasted_iota(jnp.int32, (SEGS, segments_ref.shape[1]), 0)
    member = (segments_ref[...] == seg_iota).astype(F32)
    member_b = member.astype(BF16)
    lane = lax.broadcasted_iota(jnp.int32, (SEGS, 128), 1)
    total_confs = place_ref[1]
    first_conf = place_ref[0] * local_confs
    counts = jnp.sum(member, axis=1, keepdims=True)
    message = jnp.where((lane == total_confs) & (place_ref[0] == 0), counts, 0.0)
    for conf in range(local_confs):
        cols = slice(conf * hid, (conf + 1) * hid)
        mean = (summed[:, cols] * inverse).astype(BF16)
        mean_ref[:, cols] = mean
        pre = mm(own_ref[:, cols], w_self_ref[...]) + mm(mean, w_neigh_ref[...]) + bias_ref[...]
        sigm = 1.0 / (1.0 + jnp.exp(-pre))
        hidden = pre * sigm
        slope_ref[:, cols] = w_out * (sigm * (1.0 + pre * (1.0 - sigm)))
        high, low = split_two(hidden)
        hidden_sum = mm(member_b, high) + mm(member_b, low)
        hidden_sum_ref[:, cols] = hidden_sum
        score = jnp.sum(hidden_sum * w_out, axis=1, keepdims=True)
        message = message + jnp.where(lane == first_conf + conf, score, 0.0)
    for peer in range(message_ref.shape[0]):
        message_ref[peer] = message


def gradient_kernel(
    local_confs,
    place_ref,
    received_ref,
    pairs_ref,
    segments_ref,
    own_ref,
    mean_ref,
    slope_ref,
    hidden_sum_ref,
    grads_ref,
    loss_ref,
    d_pre_ref,
):
    hid = grads_ref.shape[1]
    nodes = own_ref.shape[0]
    pair_count = pairs_ref.shape[1]
    total = jnp.sum(received_ref[...], axis=0)
    lane = lax.broadcasted_iota(jnp.int32, (SEGS, 128), 1)
    counts = jnp.sum(jnp.where(lane == place_ref[1], total, 0.0), axis=1, keepdims=True)
    root = jnp.sqrt(counts)
    scores = total / root
    seg_hot = (
        pairs_ref[0:1, :] == lax.broadcasted_iota(jnp.int32, (SEGS, pair_count), 0)
    ).astype(F32)
    conf_iota = lax.broadcasted_iota(jnp.int32, (128, pair_count), 0)
    signed = (pairs_ref[1:2, :] == conf_iota).astype(F32) - (
        pairs_ref[2:3, :] == conf_iota
    ).astype(F32)
    picked = mm_exact(scores, seg_hot, ((0,), (0,)))
    margin = jnp.maximum(0.0, 1.0 - jnp.sum(picked * signed, axis=0, keepdims=True))
    loss_ref[...] = jnp.sum(margin * margin, axis=1, keepdims=True)
    d_scores = mm_exact(seg_hot, (-2.0 * margin) * signed, ((1,), (1,))) / root
    seg_iota = lax.broadcasted_iota(jnp.int32, (SEGS, nodes), 0)
    member = (segments_ref[...] == seg_iota).astype(BF16)
    member = jnp.concatenate([member, member], axis=0)
    first_conf = place_ref[0] * local_confs
    grads = None
    d_bias = None
    d_out = None
    for conf in range(local_confs):
        cols = slice(conf * hid, (conf + 1) * hid)
        column = jnp.sum(
            jnp.where(lane == first_conf + conf, d_scores, 0.0), axis=1, keepdims=True
        )
        spread = jnp.broadcast_to(column, (SEGS, hid))
        high, low = split_two(spread)
        low, last = split_two(spread - high.astype(F32))
        d_node = mm(
            jnp.concatenate([member, member[:SEGS]], axis=0),
            jnp.concatenate([high, low, last], axis=0),
            ((0,), (0,)),
        )
        d_pre = d_node * slope_ref[:, cols]
        d_pre_b = d_pre.astype(BF16)
        d_pre_ref[:, cols] = d_pre_b
        rows = jnp.concatenate([own_ref[:, cols], mean_ref[:, cols]], axis=1)
        term = mm(rows, d_pre_b, ((0,), (0,)))
        bias_term = jnp.sum(d_pre, axis=0, keepdims=True)
        out_term = jnp.sum(spread * hidden_sum_ref[:, cols], axis=0, keepdims=True)
        grads = term if grads is None else grads + term
        d_bias = bias_term if d_bias is None else d_bias + bias_term
        d_out = out_term if d_out is None else d_out + out_term
    grads_ref[: 2 * hid] = grads
    sub = lax.broadcasted_iota(jnp.int32, (8, hid), 0)
    grads_ref[2 * hid :] = jnp.where(sub == 0, d_bias, 0.0) + jnp.where(sub == 1, d_out, 0.0)


def spread_kernel(
    local_confs,
    d_pre_ref,
    w_self_ref,
    w_neigh_ref,
    degree_ref,
    tile_high_ref,
    tile_low_ref,
    far_ref,
    near_ref,
    own_ref,
):
    hid = w_self_ref.shape[0]
    inverse = 1.0 / degree_ref[...]
    for conf in range(local_confs):
        cols = slice(conf * hid, (conf + 1) * hid)
        d_pre = d_pre_ref[:, cols]
        back = (mm(d_pre, w_neigh_ref[...], ((1,), (1,))) * inverse).astype(BF16)
        own = mm(d_pre, w_self_ref[...], ((1,), (1,)))
        pieces = [
            mm(tile_high_ref[reach], back, ((0,), (0,)))
            + mm(tile_low_ref[reach], back, ((0,), (0,)))
            for reach in range(WINDOW)
        ]
        far_ref[:, cols] = pieces[0].astype(BF16)
        near_ref[:, cols] = pieces[1].astype(BF16)
        own_ref[:, cols] = own + pieces[2]


def rounded(value):
    return lax.reduce_precision(value, 8, 7)


def packed(total, main):
    vectors = total[main:]
    high = rounded(vectors)
    middle = rounded(vectors - high)
    last = rounded(vectors - high - middle)
    return jnp.concatenate([rounded(total[:main]), high, middle, last], axis=0).astype(BF16)


def unpacked(message, main):
    message = message.astype(F32)
    extra = (message.shape[0] - main) // 3
    parts = [message[main + i * extra : main + (i + 1) * extra] for i in range(3)]
    return jnp.concatenate([message[:main], parts[0] + parts[1] + parts[2]], axis=0)


def summed_over_devices(total, main):
    for axis in ("col", "row"):
        count = lax.axis_size(axis)
        if count & (count - 1):
            total = lax.psum(total, axis)
            continue
        for step in range(count.bit_length() - 1):
            if axis == "col":
                total = total + exchanged(total, axis, 1 << step)
            else:
                message = packed(total, main)
                total = unpacked(message, main) + unpacked(
                    exchanged(message, axis, 1 << step), main
                )
    return total


def body(features, tiles, pattern, degrees, segments, pairs, w_self, w_neigh, bias, w_out):
    nodes, width = features.shape
    hid = w_self.shape[0]
    local_confs = width // hid
    rows, columns = lax.axis_size("row"), lax.axis_size("col")
    position, column = lax.axis_index("row"), lax.axis_index("col")
    far = shifted(features, "row", 2)
    near = shifted(features, "row", 1)
    ids = pattern - (position - REACH)
    place = jnp.stack([column, jnp.int32(local_confs * columns)]).astype(jnp.int32)
    degree = jnp.broadcast_to(degrees.astype(F32)[:, None], (nodes, hid))
    segment_row = segments.reshape(1, nodes)
    params = pltpu.CompilerParams(vmem_limit_bytes=LIMIT)
    mean, slope, hidden_sum, message, tile_high, tile_low = pl.pallas_call(
        functools.partial(forward_kernel, local_confs),
        out_shape=(
            jax.ShapeDtypeStruct((nodes, width), BF16),
            jax.ShapeDtypeStruct((nodes, width), F32),
            jax.ShapeDtypeStruct((SEGS, width), F32),
            jax.ShapeDtypeStruct((rows * columns, SEGS, 128), F32),
            jax.ShapeDtypeStruct((WINDOW, nodes, nodes), BF16),
            jax.ShapeDtypeStruct((WINDOW, nodes, nodes), BF16),
        ),
        in_specs=[SMEM] * 2 + [VMEM] * 10,
        out_specs=(VMEM,) * 6,
        compiler_params=params,
        name="forward",
    )(
        place,
        ids,
        features,
        near,
        far,
        tiles,
        degree,
        segment_row,
        w_self,
        w_neigh,
        bias.reshape(1, hid),
        w_out.reshape(1, hid),
    )
    received = lax.all_to_all(message, ("row", "col"), 0, 0, tiled=True)
    main = 2 * hid
    grads, loss, d_pre = pl.pallas_call(
        functools.partial(gradient_kernel, local_confs),
        out_shape=(
            jax.ShapeDtypeStruct((main + 8, hid), F32),
            jax.ShapeDtypeStruct((1, 1), F32),
            jax.ShapeDtypeStruct((nodes, width), BF16),
        ),
        in_specs=[SMEM] + [VMEM] * 7,
        out_specs=(VMEM,) * 3,
        compiler_params=params,
        name="gradient",
    )(place, received, pairs.T, segment_row, features, mean, slope, hidden_sum)
    far_piece, near_piece, own_piece = pl.pallas_call(
        functools.partial(spread_kernel, local_confs),
        out_shape=(
            jax.ShapeDtypeStruct((nodes, width), BF16),
            jax.ShapeDtypeStruct((nodes, width), BF16),
            jax.ShapeDtypeStruct((nodes, width), F32),
        ),
        in_specs=[VMEM] * 6,
        out_specs=(VMEM,) * 3,
        compiler_params=params,
        name="spread",
    )(d_pre, w_self, w_neigh, degree, tile_high, tile_low)
    gathered = (
        own_piece
        + shifted(far_piece, "row", -2).astype(F32)
        + shifted(near_piece, "row", -1).astype(F32)
    )
    scale = math.sqrt(nodes * rows / SEGS)
    node_grad = (gathered * scale).astype(BF16)
    total = summed_over_devices(grads, main)
    return (
        loss.reshape(1),
        total[:hid],
        total[hid:main],
        total[main],
        total[main + 1],
        node_grad,
    )


def solution(mesh):
    in_specs = (
        P(("groups", "row"), "col"),
        P(("groups", "row"), None, None, None),
        P(("groups", "row"), None),
        P(("groups", "row")),
        P(("groups", "row")),
        P("groups", None),
        P(),
        P(),
        P(),
        P(),
    )
    out_specs = (
        P("groups"),
        P("groups", None),
        P("groups", None),
        P("groups"),
        P("groups"),
        P(("groups", "row"), "col"),
    )
    return jax.shard_map(body, mesh=mesh, in_specs=in_specs, out_specs=out_specs, check_vma=False)
```

```python
import functools
import math

import jax
import jax.numpy as jnp
from jax import lax
from jax.experimental import pallas as pl
from jax.experimental.pallas import tpu as pltpu
from jax.sharding import PartitionSpec as P

REACH = 2
SEGS = 8
WINDOW = REACH + 1
F32 = jnp.float32
BF16 = jnp.bfloat16
HIGHEST = lax.Precision.HIGHEST
VMEM = pl.BlockSpec(memory_space=pltpu.VMEM)
SMEM = pl.BlockSpec(memory_space=pltpu.SMEM)
LIMIT = 24 << 20


def shifted(value, axis, steps):
    count = lax.axis_size(axis)
    initial, last = (max(0, -steps), min(count, count - steps))
    return lax.ppermute(value, axis, [(source, source + steps) for source in range(initial, last)])


def exchanged(value, axis, bit):
    count = lax.axis_size(axis)
    return lax.ppermute(value, axis, [(source, source ^ bit) for source in range(count)])


def mm(left, right, contract=((1,), (0,))):
    return lax.dot_general(left, right, (contract, ((), ())), preferred_element_type=F32)


def mm_exact(left, right, contract):
    return lax.dot_general(
        left, right, (contract, ((), ())), precision=HIGHEST, preferred_element_type=F32
    )


def split_two(value):
    high = value.astype(BF16)
    return high, (value - high.astype(F32)).astype(BF16)


def prepare_kernel(
    local_confs,
    ids_ref,
    own_ref,
    tiles_ref,
    degree_ref,
    segments_ref,
    w_self_ref,
    bias_ref,
    tile_high_ref,
    tile_low_ref,
    far_tile_ref,
    near_tile_ref,
    base_ref,
    summed_ref,
    inverse_ref,
):
    hid = w_self_ref.shape[0]
    nodes = own_ref.shape[0]
    inverse_ref[...] = 1.0 / jnp.broadcast_to(degree_ref[...], (nodes, nodes)).astype(F32).T
    segment_rows = jnp.broadcast_to(segments_ref[...], (16, nodes)).astype(F32).astype(BF16)
    for reach in range(WINDOW):
        total = None
        for slot in range(tiles_ref.shape[1]):
            keep = (ids_ref[0, slot] == reach).astype(F32)
            term = tiles_ref[0, slot].astype(F32) * keep
            total = term if total is None else total + term
        high, low = split_two(total)
        tile_high_ref[reach] = high
        tile_low_ref[reach] = low
        if reach < REACH:
            message = (far_tile_ref, near_tile_ref)[reach]
            message[:nodes] = high
            message[nodes : 2 * nodes] = low
            message[2 * nodes :] = segment_rows
    own = own_ref[...]
    summed_ref[...] = mm(tile_high_ref[REACH], own) + mm(tile_low_ref[REACH], own)
    for conf in range(local_confs):
        cols = slice(conf * hid, (conf + 1) * hid)
        base_ref[:, cols] = mm(own_ref[:, cols], w_self_ref[...]) + bias_ref[...]


def forward_kernel(
    local_confs,
    place_ref,
    near_ref,
    far_ref,
    tile_high_ref,
    tile_low_ref,
    base_ref,
    summed_ref,
    inverse_ref,
    segments_ref,
    w_neigh_ref,
    w_out_ref,
    mean_ref,
    slope_ref,
    hidden_sum_ref,
    message_ref,
    back_ref,
):
    hid = w_neigh_ref.shape[0]
    summed = summed_ref[...]
    for reach, panel_ref in enumerate((far_ref, near_ref)):
        panel = panel_ref[...]
        summed = summed + (mm(tile_high_ref[reach], panel) + mm(tile_low_ref[reach], panel))
    inverse = inverse_ref[...]
    w_out = w_out_ref[...]
    seg_iota = lax.broadcasted_iota(jnp.int32, (SEGS, segments_ref.shape[1]), 0)
    member = (segments_ref[...] == seg_iota).astype(F32)
    member_b = member.astype(BF16)
    lane = lax.broadcasted_iota(jnp.int32, (SEGS, 128), 1)
    total_confs = place_ref[1]
    first_conf = place_ref[0] * local_confs
    counts = jnp.sum(member, axis=1, keepdims=True)
    message = jnp.where((lane == total_confs) & (place_ref[0] == 0), counts, 0.0)
    for conf in range(local_confs):
        cols = slice(conf * hid, (conf + 1) * hid)
        mean = (summed[:, cols] * inverse).astype(BF16)
        mean_ref[:, cols] = mean
        pre = base_ref[:, cols] + mm(mean, w_neigh_ref[...])
        sigm = 1.0 / (1.0 + jnp.exp(-pre))
        hidden = pre * sigm
        slope = w_out * (sigm * (1.0 + pre * (1.0 - sigm)))
        slope_ref[:, cols] = slope
        back = mm(slope.astype(BF16), w_neigh_ref[...], ((1,), (1,))) * inverse
        back_ref[:, cols] = back.astype(BF16)
        high, low = split_two(hidden)
        hidden_sum = mm(member_b, high) + mm(member_b, low)
        hidden_sum_ref[:, cols] = hidden_sum
        score = jnp.sum(hidden_sum * w_out, axis=1, keepdims=True)
        message = message + jnp.where(lane == first_conf + conf, score, 0.0)
    for peer in range(message_ref.shape[0]):
        message_ref[peer] = message


def gradient_kernel(
    local_confs,
    place_ref,
    received_ref,
    pairs_ref,
    segments_ref,
    own_ref,
    mean_ref,
    slope_ref,
    hidden_sum_ref,
    grads_ref,
    loss_ref,
    d_pre_ref,
    parts_ref,
):
    hid = grads_ref.shape[1]
    nodes = own_ref.shape[0]
    pair_count = pairs_ref.shape[1]
    total = jnp.sum(received_ref[...], axis=0)
    lane = lax.broadcasted_iota(jnp.int32, (SEGS, 128), 1)
    counts = jnp.sum(jnp.where(lane == place_ref[1], total, 0.0), axis=1, keepdims=True)
    root = jnp.sqrt(counts)
    scores = total / root
    seg_hot = (
        pairs_ref[0:1, :] == lax.broadcasted_iota(jnp.int32, (SEGS, pair_count), 0)
    ).astype(F32)
    conf_iota = lax.broadcasted_iota(jnp.int32, (128, pair_count), 0)
    signed = (pairs_ref[1:2, :] == conf_iota).astype(F32) - (
        pairs_ref[2:3, :] == conf_iota
    ).astype(F32)
    picked = mm_exact(scores, seg_hot, ((0,), (0,)))
    margin = jnp.maximum(0.0, 1.0 - jnp.sum(picked * signed, axis=0, keepdims=True))
    loss_ref[...] = jnp.sum(margin * margin, axis=1, keepdims=True)
    d_scores = mm_exact(seg_hot, (-2.0 * margin) * signed, ((1,), (1,))) / root
    member = members(segments_ref[...])
    first_conf = place_ref[0] * local_confs
    grads = None
    d_bias = None
    d_out = None
    for conf in range(local_confs):
        cols = slice(conf * hid, (conf + 1) * hid)
        column = jnp.sum(
            jnp.where(lane == first_conf + conf, d_scores, 0.0), axis=1, keepdims=True
        )
        spread = jnp.broadcast_to(column, (SEGS, hid))
        high, low = split_two(spread)
        low, last = split_two(spread - high.astype(F32))
        parts = jnp.concatenate([high, low, last], axis=0)
        parts_ref[:, cols] = parts
        d_pre = mm(member, parts, ((0,), (0,))) * slope_ref[:, cols]
        d_pre_b = d_pre.astype(BF16)
        d_pre_ref[:, cols] = d_pre_b
        rows = jnp.concatenate([own_ref[:, cols], mean_ref[:, cols]], axis=1)
        term = mm(rows, d_pre_b, ((0,), (0,)))
        bias_term = jnp.sum(d_pre, axis=0, keepdims=True)
        out_term = jnp.sum(spread * hidden_sum_ref[:, cols], axis=0, keepdims=True)
        grads = term if grads is None else grads + term
        d_bias = bias_term if d_bias is None else d_bias + bias_term
        d_out = out_term if d_out is None else d_out + out_term
    grads_ref[: 2 * hid] = grads
    sub = lax.broadcasted_iota(jnp.int32, (8, hid), 0)
    grads_ref[2 * hid :] = jnp.where(sub == 0, d_bias, 0.0) + jnp.where(sub == 1, d_out, 0.0)


def members(segment_row):
    seg_iota = lax.broadcasted_iota(jnp.int32, (SEGS, segment_row.shape[1]), 0)
    member = (segment_row.astype(jnp.int32) == seg_iota).astype(F32)
    return jnp.concatenate([member, member, member], axis=0).astype(BF16)


def spread_kernel(
    local_confs,
    scale,
    d_pre_ref,
    parts_ref,
    w_self_ref,
    w_neigh_ref,
    inverse_ref,
    tile_high_ref,
    tile_low_ref,
    far_back_ref,
    near_back_ref,
    far_tile_ref,
    near_tile_ref,
    node_grad_ref,
):
    hid = w_self_ref.shape[0]
    nodes = d_pre_ref.shape[0]
    inverse = inverse_ref[...]
    others = []
    for back_ref, message_ref in ((far_back_ref, far_tile_ref), (near_back_ref, near_tile_ref)):
        segment_row = message_ref[2 * nodes : 2 * nodes + 16].astype(F32)[0:1]
        others.append((back_ref, message_ref, members(segment_row)))
    for conf in range(local_confs):
        cols = slice(conf * hid, (conf + 1) * hid)
        d_pre = d_pre_ref[:, cols]
        back = (mm(d_pre, w_neigh_ref[...], ((1,), (1,))) * inverse).astype(BF16)
        total = mm(d_pre, w_self_ref[...], ((1,), (1,)))
        total = total + mm(tile_high_ref[REACH], back, ((0,), (0,)))
        total = total + mm(tile_low_ref[REACH], back, ((0,), (0,)))
        for back_ref, message_ref, member in others:
            d_node = mm(member, parts_ref[:, cols], ((0,), (0,)))
            back = (d_node * back_ref[:, cols].astype(F32)).astype(BF16)
            total = total + mm(message_ref[:nodes], back, ((0,), (0,)))
            total = total + mm(message_ref[nodes : 2 * nodes], back, ((0,), (0,)))
        node_grad_ref[:, cols] = (total * scale).astype(BF16)


def rounded(value):
    return lax.reduce_precision(value, 8, 7)


def packed(total, main):
    vectors = total[main:]
    high = rounded(vectors)
    middle = rounded(vectors - high)
    last = rounded(vectors - high - middle)
    return jnp.concatenate([rounded(total[:main]), high, middle, last], axis=0).astype(BF16)


def unpacked(message, main):
    message = message.astype(F32)
    extra = (message.shape[0] - main) // 3
    parts = [message[main + i * extra : main + (i + 1) * extra] for i in range(3)]
    return jnp.concatenate([message[:main], parts[0] + parts[1] + parts[2]], axis=0)


def summed_over_devices(total, main):
    for axis in ("col", "row"):
        count = lax.axis_size(axis)
        if count & (count - 1):
            total = lax.psum(total, axis)
            continue
        for step in range(count.bit_length() - 1):
            if axis == "col":
                total = total + exchanged(total, axis, 1 << step)
            else:
                message = packed(total, main)
                total = unpacked(message, main) + unpacked(
                    exchanged(message, axis, 1 << step), main
                )
    return total


def shape(dims, dtype):
    return jax.ShapeDtypeStruct(dims, dtype)


def kernel_call(kernel, outs, scalars, name, flops, *operands):
    moved = sum(math.prod(leaf.shape) * leaf.dtype.itemsize for leaf in operands + tuple(outs))
    return pl.pallas_call(
        kernel,
        out_shape=outs,
        in_specs=[SMEM] * scalars + [VMEM] * (len(operands) - scalars),
        out_specs=(VMEM,) * len(outs),
        compiler_params=pltpu.CompilerParams(vmem_limit_bytes=LIMIT),
        cost_estimate=pl.CostEstimate(flops=flops, bytes_accessed=moved, transcendentals=0),
        name=name,
    )(*operands)


def body(features, tiles, pattern, degrees, segments, pairs, w_self, w_neigh, bias, w_out):
    nodes, width = features.shape
    hid = w_self.shape[0]
    local_confs = width // hid
    rows, columns = lax.axis_size("row"), lax.axis_size("col")
    position, column = lax.axis_index("row"), lax.axis_index("col")
    product = 2 * nodes * nodes * width
    far = shifted(features, "row", 2)
    near = shifted(features, "row", 1)
    ids = pattern - (position - REACH)
    place = jnp.stack([column, jnp.int32(local_confs * columns)]).astype(jnp.int32)
    segment_row = segments.reshape(1, nodes)
    wide = shape((nodes, width), F32)
    narrow = shape((nodes, width), BF16)
    tile_set = shape((WINDOW, nodes, nodes), BF16)
    tile_message = shape((2 * nodes + 16, nodes), BF16)
    tile_high, tile_low, far_tile, near_tile, base, summed, inverse = kernel_call(
        functools.partial(prepare_kernel, local_confs),
        (tile_set, tile_set, tile_message, tile_message, wide, wide, shape((nodes, nodes), F32)),
        1,
        "prepare",
        3 * product,
        ids,
        features,
        tiles,
        degrees.reshape(1, nodes),
        segment_row,
        w_self,
        bias.reshape(1, hid),
    )
    far_tile = shifted(far_tile, "row", -2)
    near_tile = shifted(near_tile, "row", -1)
    mean, slope, hidden_sum, message, back = kernel_call(
        functools.partial(forward_kernel, local_confs),
        (
            narrow,
            wide,
            shape((SEGS, width), F32),
            shape((rows * columns, SEGS, 128), F32),
            narrow,
        ),
        1,
        "forward",
        6 * product,
        place,
        near,
        far,
        tile_high,
        tile_low,
        base,
        summed,
        inverse,
        segment_row,
        w_neigh,
        w_out.reshape(1, hid),
    )
    far_back = shifted(back, "row", -2)
    near_back = shifted(back, "row", -1)
    received = lax.all_to_all(message, ("row", "col"), 0, 0, tiled=True)
    main = 2 * hid
    grads, loss, d_pre, parts = kernel_call(
        functools.partial(gradient_kernel, local_confs),
        (
            shape((main + 8, hid), F32),
            shape((1, 1), F32),
            narrow,
            shape((3 * SEGS, width), BF16),
        ),
        1,
        "gradient",
        3 * product,
        place,
        received,
        pairs.T,
        segment_row,
        features,
        mean,
        slope,
        hidden_sum,
    )
    scale = math.sqrt(nodes * rows / SEGS)
    (node_grad,) = kernel_call(
        functools.partial(spread_kernel, local_confs, scale),
        (narrow,),
        0,
        "spread",
        10 * product,
        d_pre,
        parts,
        w_self,
        w_neigh,
        inverse,
        tile_high,
        tile_low,
        far_back,
        near_back,
        far_tile,
        near_tile,
    )
    total = summed_over_devices(grads, main)
    return (
        loss.reshape(1),
        total[:hid],
        total[hid:main],
        total[main],
        total[main + 1],
        node_grad,
    )


def solution(mesh):
    in_specs = (
        P(("groups", "row"), "col"),
        P(("groups", "row"), None, None, None),
        P(("groups", "row"), None),
        P(("groups", "row")),
        P(("groups", "row")),
        P("groups", None),
        P(),
        P(),
        P(),
        P(),
    )
    out_specs = (
        P("groups"),
        P("groups", None),
        P("groups", None),
        P("groups"),
        P("groups"),
        P(("groups", "row"), "col"),
    )
    return jax.shard_map(body, mesh=mesh, in_specs=in_specs, out_specs=out_specs, check_vma=False)
```

```python
import functools
import math

import jax
import jax.numpy as jnp
from jax import lax
from jax.experimental import pallas as pl
from jax.experimental.pallas import tpu as pltpu
from jax.sharding import PartitionSpec as P

REACH = 2
SEGS = 8
WINDOW = REACH + 1
F32 = jnp.float32
BF16 = jnp.bfloat16
HIGHEST = lax.Precision.HIGHEST
VMEM = pl.BlockSpec(memory_space=pltpu.VMEM)
SMEM = pl.BlockSpec(memory_space=pltpu.SMEM)
LIMIT = 24 << 20


def shifted(value, axis, steps):
    count = lax.axis_size(axis)
    initial, last = (max(0, -steps), min(count, count - steps))
    return lax.ppermute(value, axis, [(source, source + steps) for source in range(initial, last)])


def exchanged(value, axis, bit):
    count = lax.axis_size(axis)
    return lax.ppermute(value, axis, [(source, source ^ bit) for source in range(count)])


def mm(left, right, contract=((1,), (0,))):
    return lax.dot_general(left, right, (contract, ((), ())), preferred_element_type=F32)


def mm_exact(left, right, contract):
    return lax.dot_general(
        left, right, (contract, ((), ())), precision=HIGHEST, preferred_element_type=F32
    )


def split_two(value):
    high = value.astype(BF16)
    return high, (value - high.astype(F32)).astype(BF16)


def split_three(value):
    high, rest = value.astype(BF16), value
    rest = rest - high.astype(F32)
    middle = rest.astype(BF16)
    return high, middle, (rest - middle.astype(F32)).astype(BF16)


def iota(dims, dim):
    return lax.broadcasted_iota(jnp.int32, dims, dim)


def column_of(row, count):
    return jnp.broadcast_to(row.astype(F32), (count, row.shape[1])).T


def prepare_kernel(
    local_confs,
    pattern_ref,
    features_ref,
    tiles_ref,
    w_self_ref,
    w_neigh_ref,
    degree_ref,
    segments_ref,
    pairs_ref,
    bias_ref,
    w_out_ref,
    own_ref,
    self_ref,
    neigh_ref,
    out_ref,
    high_ref,
    low_ref,
    base_ref,
    summed_ref,
    inverse_ref,
    expand_ref,
    mask_ref,
    chosen_ref,
    stub_ref,
    tiles_buffer,
    sems,
):
    copies = [
        pltpu.make_async_copy(source, target, sems.at[i])
        for i, (source, target) in enumerate(
            (
                (tiles_ref, tiles_buffer),
                (features_ref, own_ref),
                (w_self_ref, self_ref),
                (w_neigh_ref, neigh_ref),
            )
        )
    ]
    for copy in copies:
        copy.start()
    nodes, hid = own_ref.shape[0], self_ref.shape[0]
    first_conf = lax.axis_index("col") * local_confs
    lowest = lax.axis_index("row") - REACH
    out_ref[...] = w_out_ref[...]
    inverse_ref[...] = 1.0 / column_of(degree_ref[...], nodes)
    slots = expand_ref.shape[0]
    for conf in range(local_confs):
        cols = slice(conf * hid, (conf + 1) * hid)
        chosen = iota((slots, hid), 0) // SEGS == first_conf + conf
        expand_ref[:, cols] = chosen.astype(F32).astype(BF16)
    segment_row = segments_ref[...]
    mask = (column_of(segment_row, slots).astype(jnp.int32) == iota((nodes, slots), 1) % SEGS).astype(
        F32
    )
    mask_ref[...] = mask
    slot = iota((slots, pairs_ref.shape[1]), 0)
    segment = pairs_ref[0:1, :]
    first = (pairs_ref[1:2, :] * SEGS + segment == slot).astype(F32)
    second = (pairs_ref[2:3, :] * SEGS + segment == slot).astype(F32)
    chosen_ref[...] = (first - second).astype(BF16)
    counts = jnp.sum(mask, axis=0, keepdims=True) * (first_conf == 0).astype(F32)
    sub = iota((8, slots), 0)
    stub_ref[...] = jnp.where(sub == 1, counts, 0.0) + jnp.where(
        sub == 2, segment_row.astype(F32), 0.0
    )
    copies[0].wait()
    for reach in range(WINDOW):
        total = None
        for index in range(tiles_buffer.shape[1]):
            keep = (pattern_ref[0, index] - lowest == reach).astype(F32)
            term = tiles_buffer[0, index].astype(F32) * keep
            total = term if total is None else total + term
        high, low = split_two(total)
        high_ref[reach] = high
        low_ref[reach] = low
    copies[1].wait()
    own = own_ref[...]
    summed_ref[...] = mm(high_ref[REACH], own) + mm(low_ref[REACH], own)
    copies[2].wait()
    for conf in range(local_confs):
        cols = slice(conf * hid, (conf + 1) * hid)
        base_ref[:, cols] = mm(own_ref[:, cols], self_ref[...]) + bias_ref[...]
    copies[3].wait()


def forward_kernel(
    local_confs,
    near_ref,
    far_ref,
    neigh_ref,
    out_ref,
    high_ref,
    low_ref,
    base_ref,
    summed_ref,
    inverse_ref,
    stub_ref,
    mean_ref,
    slope_ref,
    hidden_ref,
    message_ref,
    far_back_ref,
    near_back_ref,
):
    nodes, hid = base_ref.shape[0], neigh_ref.shape[0]
    summed = summed_ref[...]
    for reach, panel_ref in enumerate((far_ref, near_ref)):
        panel = panel_ref[...]
        summed = summed + (mm(high_ref[reach], panel) + mm(low_ref[reach], panel))
    inverse = inverse_ref[...]
    w_out = out_ref[...]
    segment_row = stub_ref[2:3, :].astype(jnp.int32)
    member = (segment_row == iota((SEGS, nodes), 0)).astype(F32).astype(BF16)
    first_conf = lax.axis_index("col") * local_confs
    hidden_ref[...] = jnp.zeros_like(hidden_ref)
    for conf in range(local_confs):
        cols = slice(conf * hid, (conf + 1) * hid)
        mean = (summed[:, cols] * inverse).astype(BF16)
        mean_ref[:, cols] = mean
        pre = base_ref[:, cols] + mm(mean, neigh_ref[...])
        sigm = 1.0 / (1.0 + jnp.exp(-pre))
        hidden = pre * sigm
        slope = w_out * (sigm * (1.0 + pre * (1.0 - sigm)))
        slope_ref[:, cols] = slope
        back = (mm(slope.astype(BF16), neigh_ref[...], ((1,), (1,))) * inverse).astype(BF16)
        far_back_ref[:nodes, cols] = back
        near_back_ref[:nodes, cols] = back
        high, low = split_two(hidden)
        start = pl.multiple_of((first_conf + conf) * SEGS, SEGS)
        hidden_ref[pl.ds(start, SEGS), :] = mm(member, high) + mm(member, low)
    step = nodes // local_confs
    for part in range(local_confs):
        rows = slice(part * step, (part + 1) * step)
        cols = slice(part * nodes, (part + 1) * nodes)
        far_back_ref[nodes:, cols] = high_ref[0, rows]
        near_back_ref[nodes:, cols] = high_ref[1, rows]
    scores = mm_exact(jnp.broadcast_to(w_out, (8, hid)), hidden_ref[...], ((1,), (1,)))
    message = stub_ref[...] + jnp.where(iota(scores.shape, 0) == 0, scores, 0.0)
    for peer in range(message_ref.shape[0]):
        message_ref[peer] = message


def gradient_kernel(
    local_confs,
    received_ref,
    chosen_ref,
    mask_ref,
    expand_ref,
    own_ref,
    mean_ref,
    slope_ref,
    hidden_ref,
    grads_ref,
    loss_ref,
    d_pre_ref,
    d_row_ref,
):
    hid = grads_ref.shape[1]
    total = jnp.sum(received_ref[...], axis=0)
    root = jnp.sqrt(total[1:2])
    scores = total[0:1] / root
    chosen = chosen_ref[...]

    def one_row(row, contract):
        parts = jnp.concatenate([part.astype(F32) for part in split_three(row)], axis=0)
        parts = jnp.concatenate([parts, jnp.zeros((5, row.shape[1]), F32)], axis=0).astype(BF16)
        return jnp.sum(mm(parts, chosen, contract), axis=0, keepdims=True)

    margin = jnp.maximum(0.0, 1.0 - one_row(scores, ((1,), (0,))))
    loss_ref[...] = jnp.sum(margin * margin, axis=1, keepdims=True)
    d_row = one_row(-2.0 * margin, ((1,), (1,))) / root
    d_rows = jnp.broadcast_to(d_row, d_row_ref.shape)
    d_row_ref[...] = d_rows
    factors = split_three(mask_ref[...] * d_row)
    grads = None
    d_bias = None
    for conf in range(local_confs):
        cols = slice(conf * hid, (conf + 1) * hid)
        expand = expand_ref[:, cols]
        d_node = mm(factors[0], expand) + mm(factors[1], expand) + mm(factors[2], expand)
        d_pre = d_node * slope_ref[:, cols]
        d_pre_b = d_pre.astype(BF16)
        d_pre_ref[:, cols] = d_pre_b
        rows = jnp.concatenate([own_ref[:, cols], mean_ref[:, cols]], axis=1)
        term = mm(d_pre_b, rows, ((0,), (0,)))
        grads = term if grads is None else grads + term
        d_bias = d_pre if d_bias is None else d_bias + d_pre
    grads_ref[: 2 * hid] = grads.T
    d_out = mm_exact(d_rows, hidden_ref[...], ((1,), (0,)))
    d_bias = jnp.sum(d_bias, axis=0, keepdims=True)
    sub = iota((8, hid), 0)
    grads_ref[2 * hid :] = jnp.where(sub == 0, d_bias, 0.0) + jnp.where(sub == 1, d_out, 0.0)


def spread_kernel(
    local_confs,
    columns,
    scale,
    d_pre_ref,
    d_row_ref,
    expand_ref,
    self_ref,
    neigh_ref,
    inverse_ref,
    high_ref,
    low_ref,
    far_back_ref,
    near_back_ref,
    received_ref,
    node_grad_ref,
):
    hid = self_ref.shape[0]
    nodes = d_pre_ref.shape[0]
    slots = expand_ref.shape[0]
    inverse = inverse_ref[...]
    d_row = d_row_ref[0:1, :]
    row, column = lax.axis_index("row"), lax.axis_index("col")
    step = nodes // local_confs
    others = []
    for distance, back_ref in ((2, far_back_ref), (1, near_back_ref)):
        source = jnp.minimum(row + distance, lax.axis_size("row") - 1)
        segment_row = received_ref[source * columns + column][2:3, :]
        segment = column_of(segment_row, slots).astype(jnp.int32)
        mask = (segment == iota((nodes, slots), 1) % SEGS).astype(F32)
        tile = jnp.concatenate(
            [back_ref[nodes:, part * nodes : (part + 1) * nodes] for part in range(local_confs)],
            axis=0,
        )
        others.append((back_ref, tile, split_two(mask * d_row)))
    for conf in range(local_confs):
        cols = slice(conf * hid, (conf + 1) * hid)
        d_pre = d_pre_ref[:, cols]
        back = (mm(d_pre, neigh_ref[...], ((1,), (1,))) * inverse).astype(BF16)
        total = mm(d_pre, self_ref[...], ((1,), (1,)))
        total = total + mm(high_ref[REACH], back, ((0,), (0,)))
        total = total + mm(low_ref[REACH], back, ((0,), (0,)))
        expand = expand_ref[:, cols]
        for back_ref, tile, (high, low) in others:
            d_node = mm(high, expand) + mm(low, expand)
            back = (d_node * back_ref[:nodes, cols].astype(F32)).astype(BF16)
            total = total + mm(tile, back, ((0,), (0,)))
        node_grad_ref[:, cols] = (total * scale).astype(BF16)


def rounded(value):
    return lax.reduce_precision(value, 8, 7)


def packed(total, main):
    vectors = total[main:]
    high = rounded(vectors)
    middle = rounded(vectors - high)
    last = rounded(vectors - high - middle)
    return jnp.concatenate([rounded(total[:main]), high, middle, last], axis=0).astype(BF16)


def unpacked(message, main):
    message = message.astype(F32)
    extra = (message.shape[0] - main) // 3
    parts = [message[main + i * extra : main + (i + 1) * extra] for i in range(3)]
    return jnp.concatenate([message[:main], parts[0] + parts[1] + parts[2]], axis=0)


def summed_over_devices(total, main):
    for axis in ("col", "row"):
        count = lax.axis_size(axis)
        if count & (count - 1):
            total = lax.psum(total, axis)
            continue
        if axis == "col":
            for step in range(count.bit_length() - 1):
                total = total + exchanged(total, axis, 1 << step)
            continue
        stride = 1
        while stride < count:
            message = packed(total, main)
            others = [
                exchanged(message, axis, stride * k) for k in (1, 2, 3) if stride * k < count
            ]
            if len(others) == 1:
                total = unpacked(message, main) + unpacked(others[0], main)
            else:
                total = four_summed([unpacked(m, main) for m in [message] + others])
            stride *= 4
    return total


def four_summed(parts):
    return (parts[0] + parts[1]) + (parts[2] + parts[3])


def shape(dims, dtype):
    return jax.ShapeDtypeStruct(dims, dtype)


def kernel_call(kernel, outs, spaces, name, flops, operands, scratch=()):
    moved = sum(math.prod(leaf.shape) * leaf.dtype.itemsize for leaf in tuple(operands) + tuple(outs))
    spaces = list(spaces) + [pltpu.VMEM] * (len(operands) - len(spaces))
    return pl.pallas_call(
        kernel,
        out_shape=outs,
        in_specs=[pl.BlockSpec(memory_space=space) for space in spaces],
        out_specs=(pl.BlockSpec(memory_space=pltpu.VMEM),) * len(outs),
        scratch_shapes=scratch,
        compiler_params=pltpu.CompilerParams(vmem_limit_bytes=LIMIT),
        cost_estimate=pl.CostEstimate(flops=flops, bytes_accessed=moved, transcendentals=0),
        name=name,
    )(*operands)


def body(features, tiles, pattern, degrees, segments, pairs, w_self, w_neigh, bias, w_out):
    nodes, width = features.shape
    hid = w_self.shape[0]
    local_confs = width // hid
    rows, columns = lax.axis_size("row"), lax.axis_size("col")
    product = 2 * nodes * nodes * width
    slots = local_confs * columns * SEGS
    far = shifted(features, "row", 2)
    near = shifted(features, "row", 1)
    wide = shape((nodes, width), F32)
    narrow = shape((nodes, width), BF16)
    square = shape((nodes, nodes), F32)
    weight = shape((hid, hid), BF16)
    tile_set = shape((WINDOW, nodes, nodes), BF16)
    own, self_w, neigh_w, out_w, high, low, base, summed, inverse, expand, mask, chosen, stub = (
        kernel_call(
            functools.partial(prepare_kernel, local_confs),
            (
                narrow,
                weight,
                weight,
                shape((1, hid), F32),
                tile_set,
                tile_set,
                wide,
                wide,
                square,
                shape((slots, width), BF16),
                shape((nodes, slots), F32),
                shape((slots, pairs.shape[0]), BF16),
                shape((8, slots), F32),
            ),
            [pltpu.SMEM] + [pltpu.HBM] * 4,
            "prepare",
            3 * product,
            (
                pattern,
                features,
                tiles,
                w_self,
                w_neigh,
                degrees.reshape(1, nodes),
                segments.reshape(1, nodes),
                pairs.T,
                bias.reshape(1, hid),
                w_out.reshape(1, hid),
            ),
            (pltpu.VMEM(tiles.shape, tiles.dtype), pltpu.SemaphoreType.DMA((4,))),
        )
    )
    back_message = shape((nodes + nodes // local_confs, width), BF16)
    mean, slope, hidden, message, far_back, near_back = kernel_call(
        functools.partial(forward_kernel, local_confs),
        (
            narrow,
            wide,
            shape((slots, hid), F32),
            shape((rows * columns, 8, slots), F32),
            back_message,
            back_message,
        ),
        [],
        "forward",
        6 * product,
        (near, far, neigh_w, out_w, high, low, base, summed, inverse, stub),
    )
    far_back = shifted(far_back, "row", -2)
    near_back = shifted(near_back, "row", -1)
    received = lax.all_to_all(message, ("row", "col"), 0, 0, tiled=True)
    received, far_back, near_back = lax.optimization_barrier((received, far_back, near_back))
    main = 2 * hid
    grads, loss, d_pre, d_row = kernel_call(
        functools.partial(gradient_kernel, local_confs),
        (
            shape((main + 8, hid), F32),
            shape((1, 1), F32),
            narrow,
            shape((8, slots), F32),
        ),
        [],
        "gradient",
        3 * product,
        (received, chosen, mask, expand, own, mean, slope, hidden),
    )
    scale = math.sqrt(nodes * rows / SEGS)
    (node_grad,) = kernel_call(
        functools.partial(spread_kernel, local_confs, columns, scale),
        (narrow,),
        [],
        "spread",
        10 * product,
        (
            d_pre,
            d_row,
            expand,
            self_w,
            neigh_w,
            inverse,
            high,
            low,
            far_back,
            near_back,
            received,
        ),
    )
    total = summed_over_devices(grads, main)
    return (
        loss.reshape(1),
        total[:hid],
        total[hid:main],
        total[main],
        total[main + 1],
        node_grad,
    )


def solution(mesh):
    in_specs = (
        P(("groups", "row"), "col"),
        P(("groups", "row"), None, None, None),
        P(("groups", "row"), None),
        P(("groups", "row")),
        P(("groups", "row")),
        P("groups", None),
        P(),
        P(),
        P(),
        P(),
    )
    out_specs = (
        P("groups"),
        P("groups", None),
        P("groups", None),
        P("groups"),
        P("groups"),
        P(("groups", "row"), "col"),
    )
    return jax.shard_map(body, mesh=mesh, in_specs=in_specs, out_specs=out_specs, check_vma=False)
```

```python
import functools
import math

import jax
import jax.numpy as jnp
from jax import lax
from jax.experimental import pallas as pl
from jax.experimental.pallas import tpu as pltpu
from jax.sharding import PartitionSpec as P

REACH = 2
SEGS = 8
WINDOW = REACH + 1
F32 = jnp.float32
BF16 = jnp.bfloat16
HIGHEST = lax.Precision.HIGHEST
VMEM = pl.BlockSpec(memory_space=pltpu.VMEM)
SMEM = pl.BlockSpec(memory_space=pltpu.SMEM)
LIMIT = 24 << 20


def shifted(value, axis, steps):
    count = lax.axis_size(axis)
    initial, last = (max(0, -steps), min(count, count - steps))
    return lax.ppermute(value, axis, [(source, source + steps) for source in range(initial, last)])


def exchanged(value, axis, bit):
    count = lax.axis_size(axis)
    return lax.ppermute(value, axis, [(source, source ^ bit) for source in range(count)])


def mm(left, right, contract=((1,), (0,))):
    return lax.dot_general(left, right, (contract, ((), ())), preferred_element_type=F32)


def mm_exact(left, right, contract):
    return lax.dot_general(
        left, right, (contract, ((), ())), precision=HIGHEST, preferred_element_type=F32
    )


def split_two(value):
    high = value.astype(BF16)
    return high, (value - high.astype(F32)).astype(BF16)


def split_three(value):
    high, rest = value.astype(BF16), value
    rest = rest - high.astype(F32)
    middle = rest.astype(BF16)
    return high, middle, (rest - middle.astype(F32)).astype(BF16)


def sigmoid(value):
    return 0.5 + 0.5 * jnp.tanh(0.5 * value)


def iota(dims, dim):
    return lax.broadcasted_iota(jnp.int32, dims, dim)


def column_of(row, count):
    return jnp.broadcast_to(row.astype(F32), (count, row.shape[1])).T


def parcel_kernel(
    local_confs,
    pattern_ref,
    features_ref,
    tiles_ref,
    degree_ref,
    segments_ref,
    own_ref,
    high_ref,
    low_ref,
    payload_ref,
    tiles_buffer,
    sems,
):
    copies = [
        pltpu.make_async_copy(source, target, sems.at[i])
        for i, (source, target) in enumerate(((tiles_ref, tiles_buffer), (features_ref, own_ref)))
    ]
    for copy in copies:
        copy.start()
    nodes = own_ref.shape[0]
    lowest = lax.axis_index("row") - REACH
    step = nodes // local_confs
    segment_row = segments_ref[...]
    notes = jnp.where(iota((8, nodes), 0) == 0, segment_row, degree_ref[...])
    notes = notes.astype(F32).astype(BF16)
    payload_ref[nodes + WINDOW * step :] = jnp.concatenate([notes] * local_confs, axis=1)
    copies[0].wait()
    for reach in range(WINDOW):
        total = None
        for index in range(tiles_buffer.shape[1]):
            keep = (pattern_ref[0, index] - lowest == reach).astype(F32)
            term = tiles_buffer[0, index].astype(F32) * keep
            total = term if total is None else total + term
        high, low = split_two(total)
        high_ref[reach] = high
        low_ref[reach] = low
        rows = slice(nodes + reach * step, nodes + (reach + 1) * step)
        for part in range(local_confs):
            payload_ref[rows, part * nodes : (part + 1) * nodes] = high[
                part * step : (part + 1) * step
            ]
    copies[1].wait()
    payload_ref[:nodes] = own_ref[...]


def prepare_kernel(
    local_confs,
    self_w_ref,
    neigh_w_ref,
    own_ref,
    high_ref,
    low_ref,
    degree_ref,
    segments_ref,
    pairs_ref,
    bias_ref,
    w_out_ref,
    self_ref,
    neigh_ref,
    out_ref,
    bias_out_ref,
    base_ref,
    summed_ref,
    inverse_ref,
    expand_ref,
    mask_ref,
    chosen_ref,
    stub_ref,
    sems,
):
    copies = [
        pltpu.make_async_copy(source, target, sems.at[i])
        for i, (source, target) in enumerate(((self_w_ref, self_ref), (neigh_w_ref, neigh_ref)))
    ]
    for copy in copies:
        copy.start()
    nodes, hid = own_ref.shape[0], self_ref.shape[0]
    first_conf = lax.axis_index("col") * local_confs
    out_ref[...] = w_out_ref[...]
    bias_out_ref[...] = bias_ref[...]
    inverse_ref[...] = 1.0 / column_of(degree_ref[...], nodes)
    slots = expand_ref.shape[0]
    for conf in range(local_confs):
        cols = slice(conf * hid, (conf + 1) * hid)
        chosen = iota((slots, hid), 0) // SEGS == first_conf + conf
        expand_ref[:, cols] = chosen.astype(F32).astype(BF16)
    segment_row = segments_ref[...]
    segment = column_of(segment_row, slots).astype(jnp.int32)
    mask = (segment == iota((nodes, slots), 1) % SEGS).astype(F32)
    mask_ref[...] = mask
    slot = iota((slots, pairs_ref.shape[1]), 0)
    segment = pairs_ref[0:1, :]
    first = (pairs_ref[1:2, :] * SEGS + segment == slot).astype(F32)
    second = (pairs_ref[2:3, :] * SEGS + segment == slot).astype(F32)
    chosen_ref[...] = (first - second).astype(BF16)
    counts = jnp.sum(mask, axis=0, keepdims=True) * (first_conf == 0).astype(F32)
    sub = iota((8, slots), 0)
    stub_ref[...] = jnp.where(sub == 1, counts, 0.0) + jnp.where(
        sub == 2, segment_row.astype(F32), 0.0
    )
    own = own_ref[...]
    summed_ref[...] = mm(high_ref[REACH], own) + mm(low_ref[REACH], own)
    copies[0].wait()
    for conf in range(local_confs):
        cols = slice(conf * hid, (conf + 1) * hid)
        base_ref[:, cols] = mm(own_ref[:, cols], self_ref[...]) + bias_ref[...]
    copies[1].wait()


def forward_kernel(
    local_confs,
    near_ref,
    far_ref,
    neigh_ref,
    out_ref,
    high_ref,
    low_ref,
    base_ref,
    summed_ref,
    inverse_ref,
    stub_ref,
    mean_ref,
    slope_ref,
    hidden_ref,
    message_ref,
):
    nodes, hid = base_ref.shape[0], neigh_ref.shape[0]
    summed = summed_ref[...]
    for reach, panel_ref in enumerate((far_ref, near_ref)):
        panel = panel_ref[...]
        summed = summed + (mm(high_ref[reach], panel) + mm(low_ref[reach], panel))
    inverse = inverse_ref[...]
    w_out = out_ref[...]
    segment_row = stub_ref[2:3, :].astype(jnp.int32)
    member = (segment_row == iota((SEGS, nodes), 0)).astype(F32).astype(BF16)
    first_conf = lax.axis_index("col") * local_confs
    hidden_ref[...] = jnp.zeros_like(hidden_ref)
    for conf in range(local_confs):
        cols = slice(conf * hid, (conf + 1) * hid)
        mean = (summed[:, cols] * inverse).astype(BF16)
        mean_ref[:, cols] = mean
        pre = base_ref[:, cols] + mm(mean, neigh_ref[...])
        sigm = sigmoid(pre)
        hidden = pre * sigm
        slope = w_out * (sigm * (1.0 + pre * (1.0 - sigm)))
        slope_ref[:, cols] = slope
        high, low = split_two(hidden)
        start = pl.multiple_of((first_conf + conf) * SEGS, SEGS)
        hidden_ref[pl.ds(start, SEGS), :] = mm(member, high) + mm(member, low)
    scores = mm_exact(jnp.broadcast_to(w_out, (8, hid)), hidden_ref[...], ((1,), (1,)))
    message = stub_ref[...] + jnp.where(iota(scores.shape, 0) == 0, scores, 0.0)
    for peer in range(message_ref.shape[0]):
        message_ref[peer] = message


def gradient_kernel(
    local_confs,
    received_ref,
    chosen_ref,
    mask_ref,
    expand_ref,
    own_ref,
    mean_ref,
    slope_ref,
    hidden_ref,
    grads_ref,
    loss_ref,
    d_pre_ref,
    d_row_ref,
):
    hid = grads_ref.shape[1]
    total = jnp.sum(received_ref[...], axis=0)
    root = jnp.sqrt(total[1:2])
    scores = total[0:1] / root
    chosen = chosen_ref[...]

    def one_row(row, contract):
        parts = jnp.concatenate([part.astype(F32) for part in split_three(row)], axis=0)
        parts = jnp.concatenate([parts, jnp.zeros((5, row.shape[1]), F32)], axis=0).astype(BF16)
        return jnp.sum(mm(parts, chosen, contract), axis=0, keepdims=True)

    margin = jnp.maximum(0.0, 1.0 - one_row(scores, ((1,), (0,))))
    loss_ref[...] = jnp.sum(margin * margin, axis=1, keepdims=True)
    d_row = one_row(-2.0 * margin, ((1,), (1,))) / root
    d_rows = jnp.broadcast_to(d_row, d_row_ref.shape)
    d_row_ref[...] = d_rows
    factors = split_three(mask_ref[...] * d_row)
    grads = None
    d_bias = None
    for conf in range(local_confs):
        cols = slice(conf * hid, (conf + 1) * hid)
        expand = expand_ref[:, cols]
        d_node = mm(factors[0], expand) + mm(factors[1], expand) + mm(factors[2], expand)
        d_pre = d_node * slope_ref[:, cols]
        d_pre_b = d_pre.astype(BF16)
        d_pre_ref[:, cols] = d_pre_b
        rows = jnp.concatenate([own_ref[:, cols], mean_ref[:, cols]], axis=1)
        term = mm(d_pre_b, rows, ((0,), (0,)))
        grads = term if grads is None else grads + term
        d_bias = d_pre if d_bias is None else d_bias + d_pre
    grads_ref[: 2 * hid] = grads.T
    d_out = mm_exact(d_rows, hidden_ref[...], ((1,), (0,)))
    d_bias = jnp.sum(d_bias, axis=0, keepdims=True)
    sub = iota((8, hid), 0)
    grads_ref[2 * hid :] = jnp.where(sub == 0, d_bias, 0.0) + jnp.where(sub == 1, d_out, 0.0)


def own_kernel(
    local_confs,
    d_pre_ref,
    self_ref,
    neigh_ref,
    inverse_ref,
    high_ref,
    low_ref,
    total_ref,
):
    hid = self_ref.shape[0]
    inverse = inverse_ref[...]
    for conf in range(local_confs):
        cols = slice(conf * hid, (conf + 1) * hid)
        d_pre = d_pre_ref[:, cols]
        back = (mm(d_pre, neigh_ref[...], ((1,), (1,))) * inverse).astype(BF16)
        total = mm(d_pre, self_ref[...], ((1,), (1,)))
        total = total + mm(high_ref[REACH], back, ((0,), (0,)))
        total_ref[:, cols] = total + mm(low_ref[REACH], back, ((0,), (0,)))


def later_kernel(
    local_confs,
    distance,
    scale,
    d_row_ref,
    total_ref,
    first_ref,
    second_ref,
    third_ref,
    expand_ref,
    self_ref,
    neigh_ref,
    out_ref,
    bias_ref,
    result_ref,
):
    hid = self_ref.shape[0]
    nodes = total_ref.shape[0]
    slots = expand_ref.shape[0]
    step = nodes // local_confs
    notes = third_ref[nodes + WINDOW * step :, :nodes].astype(F32)
    segment = column_of(notes[0:1], slots).astype(jnp.int32)
    inverse = 1.0 / jnp.maximum(column_of(notes[1:2], nodes), 1.0)
    mask = (segment == iota((nodes, slots), 1) % SEGS).astype(F32)
    factors = split_two(mask * d_row_ref[0:1, :])
    tiles = []
    for reach in range(WINDOW):
        rows = slice(nodes + reach * step, nodes + (reach + 1) * step)
        parts = [third_ref[rows, part * nodes : (part + 1) * nodes] for part in range(local_confs)]
        tiles.append(jnp.concatenate(parts, axis=0))
    w_out = out_ref[...]
    for conf in range(local_confs):
        cols = slice(conf * hid, (conf + 1) * hid)
        own = third_ref[:nodes, cols]
        summed = mm(tiles[0], first_ref[:nodes, cols]) + mm(tiles[1], second_ref[:nodes, cols])
        mean = ((summed + mm(tiles[2], own)) * inverse).astype(BF16)
        pre = mm(own, self_ref[...]) + mm(mean, neigh_ref[...]) + bias_ref[...]
        sigm = sigmoid(pre)
        slope = w_out * (sigm * (1.0 + pre * (1.0 - sigm)))
        expand = expand_ref[:, cols]
        d_node = mm(factors[0], expand) + mm(factors[1], expand)
        d_pre = (d_node * slope).astype(BF16)
        back = (mm(d_pre, neigh_ref[...], ((1,), (1,))) * inverse).astype(BF16)
        total = total_ref[:, cols] + mm(tiles[REACH - distance], back, ((0,), (0,)))
        result_ref[:, cols] = (total * scale).astype(result_ref.dtype)


def final_kernel(main, count, *refs):
    hid = refs[0].shape[1]
    parts = [ref[...].astype(F32) for ref in refs[:count]]
    if count == 4:
        total = (parts[0] + parts[1]) + (parts[2] + parts[3])
    else:
        total = parts[0] + parts[1]
    self_ref, neigh_ref, bias_ref, out_ref = refs[count:]
    self_ref[...] = total[:hid]
    neigh_ref[...] = total[hid:main]
    extra = (total.shape[0] - main) // 3
    rows = [vectors(part, main, extra) for part in parts]
    if count == 4:
        row = (rows[0] + rows[1]) + (rows[2] + rows[3])
    else:
        row = rows[0] + rows[1]
    bias_ref[...] = row[0:1]
    out_ref[...] = row[1:2]


def vectors(message, main, extra):
    high, middle, last = (
        message[main + i * extra : main + (i + 1) * extra] for i in range(3)
    )
    return high + middle + last


def rounded(value):
    return lax.reduce_precision(value, 8, 7)


def packed(total, main):
    vectors = total[main:]
    high = rounded(vectors)
    middle = rounded(vectors - high)
    last = rounded(vectors - high - middle)
    return jnp.concatenate([rounded(total[:main]), high, middle, last], axis=0).astype(BF16)


def unpacked(message, main):
    message = message.astype(F32)
    extra = (message.shape[0] - main) // 3
    parts = [message[main + i * extra : main + (i + 1) * extra] for i in range(3)]
    return jnp.concatenate([message[:main], parts[0] + parts[1] + parts[2]], axis=0)


def row_stages(count):
    stride = 1
    while stride < count:
        yield [stride * k for k in (1, 2, 3) if stride * k < count]
        stride *= 4


def finished(parts, main, hid):
    outs = (shape((hid, hid), F32), shape((hid, hid), F32), shape((1, hid), F32), shape((1, hid), F32))
    return kernel_call(
        functools.partial(final_kernel, main, len(parts)), outs, [], "finish", 1 << 20, parts
    )


def four_summed(parts):
    return (parts[0] + parts[1]) + (parts[2] + parts[3])


def shape(dims, dtype):
    return jax.ShapeDtypeStruct(dims, dtype)


def kernel_call(kernel, outs, spaces, name, flops, operands, scratch=()):
    moved = sum(math.prod(leaf.shape) * leaf.dtype.itemsize for leaf in tuple(operands) + tuple(outs))
    spaces = list(spaces) + [pltpu.VMEM] * (len(operands) - len(spaces))
    return pl.pallas_call(
        kernel,
        out_shape=outs,
        in_specs=[pl.BlockSpec(memory_space=space) for space in spaces],
        out_specs=(pl.BlockSpec(memory_space=pltpu.VMEM),) * len(outs),
        scratch_shapes=scratch,
        compiler_params=pltpu.CompilerParams(vmem_limit_bytes=LIMIT),
        cost_estimate=pl.CostEstimate(flops=flops, bytes_accessed=moved, transcendentals=0),
        name=name,
    )(*operands)


def body(features, tiles, pattern, degrees, segments, pairs, w_self, w_neigh, bias, w_out):
    nodes, width = features.shape
    hid = w_self.shape[0]
    local_confs = width // hid
    rows, columns = lax.axis_size("row"), lax.axis_size("col")
    product = 2 * nodes * nodes * width
    slots = local_confs * columns * SEGS
    far = shifted(features, "row", 2)
    near = shifted(features, "row", 1)
    wide = shape((nodes, width), F32)
    narrow = shape((nodes, width), BF16)
    square = shape((nodes, nodes), F32)
    weight = shape((hid, hid), BF16)
    tile_set = shape((WINDOW, nodes, nodes), BF16)
    degree_row, segment_row = degrees.reshape(1, nodes), segments.reshape(1, nodes)
    in_hbm = [
        pltpu.with_memory_space_constraint(value, pltpu.HBM)
        for value in (features, tiles, w_self, w_neigh)
    ]
    own, high, low, payload = kernel_call(
        functools.partial(parcel_kernel, local_confs),
        (
            narrow,
            tile_set,
            tile_set,
            shape((nodes + WINDOW * (nodes // local_confs) + 8, width), BF16),
        ),
        [pltpu.SMEM] + [pltpu.HBM] * 2,
        "parcel",
        product,
        (pattern, in_hbm[0], in_hbm[1], degree_row, segment_row),
        (pltpu.VMEM(tiles.shape, tiles.dtype), pltpu.SemaphoreType.DMA((2,))),
    )
    (
        self_w,
        neigh_w,
        out_w,
        bias_w,
        base,
        summed,
        inverse,
        expand,
        mask,
        chosen,
        stub,
    ) = kernel_call(
        functools.partial(prepare_kernel, local_confs),
        (
            weight,
            weight,
            shape((1, hid), F32),
            shape((1, hid), F32),
            wide,
            wide,
            square,
            shape((slots, width), BF16),
            shape((nodes, slots), F32),
            shape((slots, pairs.shape[0]), BF16),
            shape((8, slots), F32),
        ),
        [pltpu.HBM] * 2,
        "prepare",
        3 * product,
        (
            in_hbm[2],
            in_hbm[3],
            own,
            high,
            low,
            degree_row,
            segment_row,
            pairs.T,
            bias.reshape(1, hid),
            w_out.reshape(1, hid),
        ),
        (pltpu.SemaphoreType.DMA((2,)),),
    )
    next_one = shifted(payload, "row", -1)
    mean, slope, hidden, message = kernel_call(
        functools.partial(forward_kernel, local_confs),
        (
            narrow,
            wide,
            shape((slots, hid), F32),
            shape((rows * columns, 8, slots), F32),
        ),
        [],
        "forward",
        6 * product,
        (near, far, neigh_w, out_w, high, low, base, summed, inverse, stub),
    )
    next_two = shifted(payload, "row", -2)
    received = lax.all_to_all(message, ("row", "col"), 0, 0, tiled=True)
    received, next_one, next_two = lax.optimization_barrier((received, next_one, next_two))
    main = 2 * hid
    grads, loss, d_pre, d_row = kernel_call(
        functools.partial(gradient_kernel, local_confs),
        (
            shape((main + 8, hid), F32),
            shape((1, 1), F32),
            narrow,
            shape((8, slots), F32),
        ),
        [],
        "gradient",
        3 * product,
        (received, chosen, mask, expand, own, mean, slope, hidden),
    )
    scale = math.sqrt(nodes * rows / SEGS)
    (node_total,) = kernel_call(
        functools.partial(own_kernel, local_confs),
        (wide,),
        [],
        "own",
        4 * product,
        (d_pre, self_w, neigh_w, inverse, high, low),
    )

    def later(distance, d_row, node_total, panels, out, factor):
        (result,) = kernel_call(
            functools.partial(later_kernel, local_confs, distance, factor),
            (out,),
            [],
            f"later{distance}",
            10 * product,
            (d_row, node_total, *panels, expand, self_w, neigh_w, out_w, bias_w),
        )
        return result

    total = grads
    for step in range(columns.bit_length() - 1):
        total = total + exchanged(total, "col", 1 << step)
    total, d_row, node_total = lax.optimization_barrier((total, d_row, node_total))
    node_total = later(1, d_row, node_total, (near, own, next_one), wide, 1.0)
    stages = list(row_stages(rows))
    for index, stage in enumerate(stages):
        packet = packed(total, main)
        parts = [packet] + [exchanged(packet, "row", bits) for bits in stage]
        if index == len(stages) - 1:
            break
        total = [unpacked(part, main) for part in parts]
        total = four_summed(total) if len(total) == 4 else total[0] + total[1]
        if index == len(stages) - 2:
            total, d_row, node_total = lax.optimization_barrier((total, d_row, node_total))
    grad_self, grad_neigh, grad_bias, grad_out = finished(parts, main, hid)
    node_grad = later(2, d_row, node_total, (own, next_one, next_two), narrow, scale)
    return (
        loss.reshape(1),
        grad_self,
        grad_neigh,
        grad_bias.reshape(hid),
        grad_out.reshape(hid),
        node_grad,
    )


def solution(mesh):
    in_specs = (
        P(("groups", "row"), "col"),
        P(("groups", "row"), None, None, None),
        P(("groups", "row"), None),
        P(("groups", "row")),
        P(("groups", "row")),
        P("groups", None),
        P(),
        P(),
        P(),
        P(),
    )
    out_specs = (
        P("groups"),
        P("groups", None),
        P("groups", None),
        P("groups"),
        P("groups"),
        P(("groups", "row"), "col"),
    )
    return jax.shard_map(body, mesh=mesh, in_specs=in_specs, out_specs=out_specs, check_vma=False)
```

```python
import functools
import math

import jax
import jax.numpy as jnp
from jax import lax
from jax.experimental import pallas as pl
from jax.experimental.pallas import tpu as pltpu
from jax.sharding import PartitionSpec as P

REACH = 2
SEGS = 8
WINDOW = REACH + 1
F32 = jnp.float32
BF16 = jnp.bfloat16
HIGHEST = lax.Precision.HIGHEST
VMEM = pl.BlockSpec(memory_space=pltpu.VMEM)
SMEM = pl.BlockSpec(memory_space=pltpu.SMEM)
LIMIT = 24 << 20


def paired(value, steps, phase):
    rows, groups = lax.axis_size("row"), lax.axis_size("groups")
    route = []
    for group in range(groups):
        for row in range(rows):
            target = row + steps if row // steps % 2 == phase else row - steps
            other = group
            if not 0 <= target < rows:
                target = row
                other = group ^ 1 if groups % 2 == 0 else group
            route.append((group * rows + row, other * rows + target))
    return lax.ppermute(value, ("groups", "row"), route)


def shifted(value, axis, steps):
    count = lax.axis_size(axis)
    initial, last = (max(0, -steps), min(count, count - steps))
    return lax.ppermute(value, axis, [(source, source + steps) for source in range(initial, last)])


def around(value):
    order = ((2, 0), (2, 1), (1, 1), (1, 0))
    found = {where: paired(value, *where) for where in order}
    return tuple(found[steps, phase] for steps in (1, 2) for phase in (0, 1))


def panels(steps, first, second):
    even = lax.axis_index("row") // steps % 2 == 0
    return jnp.where(even, second, first), jnp.where(even, first, second)


def exchanged(value, axis, bit):
    count = lax.axis_size(axis)
    return lax.ppermute(value, axis, [(source, source ^ bit) for source in range(count)])


def mm(left, right, contract=((1,), (0,))):
    return lax.dot_general(left, right, (contract, ((), ())), preferred_element_type=F32)


def mm_exact(left, right, contract):
    return lax.dot_general(
        left, right, (contract, ((), ())), precision=HIGHEST, preferred_element_type=F32
    )


def split_two(value):
    high = value.astype(BF16)
    return high, (value - high.astype(F32)).astype(BF16)


def split_three(value):
    high, rest = value.astype(BF16), value
    rest = rest - high.astype(F32)
    middle = rest.astype(BF16)
    return high, middle, (rest - middle.astype(F32)).astype(BF16)


def sigmoid(value):
    return 0.5 + 0.5 * jnp.tanh(0.5 * value)


def iota(dims, dim):
    return lax.broadcasted_iota(jnp.int32, dims, dim)


def column_of(row, count):
    return jnp.broadcast_to(row.astype(F32), (count, row.shape[1])).T


def parcel_kernel(
    local_confs,
    pattern_ref,
    features_ref,
    tiles_ref,
    degree_ref,
    segments_ref,
    own_ref,
    high_ref,
    low_ref,
    payload_ref,
    tiles_buffer,
    sems,
):
    copies = [
        pltpu.make_async_copy(source, target, sems.at[i])
        for i, (source, target) in enumerate(((tiles_ref, tiles_buffer), (features_ref, own_ref)))
    ]
    for copy in copies:
        copy.start()
    nodes = own_ref.shape[0]
    lowest = lax.axis_index("row") - REACH
    step = nodes // local_confs
    segment_row = segments_ref[...]
    notes = jnp.where(iota((8, nodes), 0) == 0, segment_row, degree_ref[...])
    notes = notes.astype(F32).astype(BF16)
    payload_ref[WINDOW * step :] = jnp.concatenate([notes] * local_confs, axis=1)
    copies[0].wait()
    for reach in range(WINDOW):
        total = None
        for index in range(tiles_buffer.shape[1]):
            keep = (pattern_ref[0, index] - lowest == reach).astype(F32)
            term = tiles_buffer[0, index].astype(F32) * keep
            total = term if total is None else total + term
        high, low = split_two(total)
        high_ref[reach] = high
        low_ref[reach] = low
        rows = slice(reach * step, (reach + 1) * step)
        for part in range(local_confs):
            payload_ref[rows, part * nodes : (part + 1) * nodes] = high[
                part * step : (part + 1) * step
            ]
    copies[1].wait()


def prepare_kernel(
    local_confs,
    self_w_ref,
    neigh_w_ref,
    own_ref,
    high_ref,
    low_ref,
    degree_ref,
    segments_ref,
    pairs_ref,
    bias_ref,
    w_out_ref,
    self_ref,
    neigh_ref,
    out_ref,
    bias_out_ref,
    base_ref,
    summed_ref,
    inverse_ref,
    expand_ref,
    mask_ref,
    chosen_ref,
    stub_ref,
    sems,
):
    copies = [
        pltpu.make_async_copy(source, target, sems.at[i])
        for i, (source, target) in enumerate(((self_w_ref, self_ref), (neigh_w_ref, neigh_ref)))
    ]
    for copy in copies:
        copy.start()
    nodes, hid = own_ref.shape[0], self_ref.shape[0]
    first_conf = lax.axis_index("col") * local_confs
    out_ref[...] = w_out_ref[...]
    bias_out_ref[...] = bias_ref[...]
    inverse_ref[...] = 1.0 / column_of(degree_ref[...], nodes)
    slots = expand_ref.shape[0]
    for conf in range(local_confs):
        cols = slice(conf * hid, (conf + 1) * hid)
        chosen = iota((slots, hid), 0) // SEGS == first_conf + conf
        expand_ref[:, cols] = chosen.astype(F32).astype(BF16)
    segment_row = segments_ref[...]
    segment = column_of(segment_row, slots).astype(jnp.int32)
    mask = (segment == iota((nodes, slots), 1) % SEGS).astype(F32)
    mask_ref[...] = mask
    slot = iota((slots, pairs_ref.shape[1]), 0)
    segment = pairs_ref[0:1, :]
    first = (pairs_ref[1:2, :] * SEGS + segment == slot).astype(F32)
    second = (pairs_ref[2:3, :] * SEGS + segment == slot).astype(F32)
    chosen_ref[...] = (first - second).astype(BF16)
    counts = jnp.sum(mask, axis=0, keepdims=True) * (first_conf == 0).astype(F32)
    sub = iota((8, slots), 0)
    stub_ref[...] = jnp.where(sub == 1, counts, 0.0) + jnp.where(
        sub == 2, segment_row.astype(F32), 0.0
    )
    own = own_ref[...]
    summed_ref[...] = mm(high_ref[REACH], own) + mm(low_ref[REACH], own)
    copies[0].wait()
    for conf in range(local_confs):
        cols = slice(conf * hid, (conf + 1) * hid)
        base_ref[:, cols] = mm(own_ref[:, cols], self_ref[...]) + bias_ref[...]
    copies[1].wait()


def forward_kernel(
    local_confs,
    near_a_ref,
    near_b_ref,
    far_a_ref,
    far_b_ref,
    neigh_ref,
    out_ref,
    high_ref,
    low_ref,
    base_ref,
    summed_ref,
    inverse_ref,
    stub_ref,
    mean_ref,
    slope_ref,
    hidden_ref,
    message_ref,
):
    nodes, hid = base_ref.shape[0], neigh_ref.shape[0]
    summed = summed_ref[...]
    far = panels(2, far_a_ref[...], far_b_ref[...])[0]
    near = panels(1, near_a_ref[...], near_b_ref[...])[0]
    for reach, panel in enumerate((far, near)):
        summed = summed + (mm(high_ref[reach], panel) + mm(low_ref[reach], panel))
    inverse = inverse_ref[...]
    w_out = out_ref[...]
    segment_row = stub_ref[2:3, :].astype(jnp.int32)
    member = (segment_row == iota((SEGS, nodes), 0)).astype(F32).astype(BF16)
    first_conf = lax.axis_index("col") * local_confs
    hidden_ref[...] = jnp.zeros_like(hidden_ref)
    for conf in range(local_confs):
        cols = slice(conf * hid, (conf + 1) * hid)
        mean = (summed[:, cols] * inverse).astype(BF16)
        mean_ref[:, cols] = mean
        pre = base_ref[:, cols] + mm(mean, neigh_ref[...])
        sigm = sigmoid(pre)
        hidden = pre * sigm
        slope = w_out * (sigm * (1.0 + pre * (1.0 - sigm)))
        slope_ref[:, cols] = slope
        high, low = split_two(hidden)
        start = pl.multiple_of((first_conf + conf) * SEGS, SEGS)
        hidden_ref[pl.ds(start, SEGS), :] = mm(member, high) + mm(member, low)
    scores = mm_exact(jnp.broadcast_to(w_out, (8, hid)), hidden_ref[...], ((1,), (1,)))
    message = stub_ref[...] + jnp.where(iota(scores.shape, 0) == 0, scores, 0.0)
    for peer in range(message_ref.shape[0]):
        message_ref[peer] = message


def gradient_kernel(
    local_confs,
    received_ref,
    chosen_ref,
    mask_ref,
    expand_ref,
    own_ref,
    mean_ref,
    slope_ref,
    hidden_ref,
    grads_ref,
    loss_ref,
    d_pre_ref,
    d_row_ref,
):
    hid = grads_ref.shape[1]
    total = jnp.sum(received_ref[...], axis=0)
    root = jnp.sqrt(total[1:2])
    scores = total[0:1] / root
    chosen = chosen_ref[...]

    def one_row(row, contract):
        parts = jnp.concatenate([part.astype(F32) for part in split_three(row)], axis=0)
        parts = jnp.concatenate([parts, jnp.zeros((5, row.shape[1]), F32)], axis=0).astype(BF16)
        return jnp.sum(mm(parts, chosen, contract), axis=0, keepdims=True)

    margin = jnp.maximum(0.0, 1.0 - one_row(scores, ((1,), (0,))))
    loss_ref[...] = jnp.sum(margin * margin, axis=1, keepdims=True)
    d_row = one_row(-2.0 * margin, ((1,), (1,))) / root
    d_rows = jnp.broadcast_to(d_row, d_row_ref.shape)
    d_row_ref[...] = d_rows
    factors = split_three(mask_ref[...] * d_row)
    grads = None
    d_bias = None
    for conf in range(local_confs):
        cols = slice(conf * hid, (conf + 1) * hid)
        expand = expand_ref[:, cols]
        d_node = mm(factors[0], expand) + mm(factors[1], expand) + mm(factors[2], expand)
        d_pre = d_node * slope_ref[:, cols]
        d_pre_b = d_pre.astype(BF16)
        d_pre_ref[:, cols] = d_pre_b
        rows = jnp.concatenate([own_ref[:, cols], mean_ref[:, cols]], axis=1)
        term = mm(d_pre_b, rows, ((0,), (0,)))
        grads = term if grads is None else grads + term
        d_bias = d_pre if d_bias is None else d_bias + d_pre
    grads_ref[: 2 * hid] = grads.T
    d_out = mm_exact(d_rows, hidden_ref[...], ((1,), (0,)))
    d_bias = jnp.sum(d_bias, axis=0, keepdims=True)
    sub = iota((8, hid), 0)
    grads_ref[2 * hid :] = jnp.where(sub == 0, d_bias, 0.0) + jnp.where(sub == 1, d_out, 0.0)


def own_kernel(
    local_confs,
    d_pre_ref,
    self_ref,
    neigh_ref,
    inverse_ref,
    high_ref,
    low_ref,
    total_ref,
):
    hid = self_ref.shape[0]
    inverse = inverse_ref[...]
    for conf in range(local_confs):
        cols = slice(conf * hid, (conf + 1) * hid)
        d_pre = d_pre_ref[:, cols]
        back = (mm(d_pre, neigh_ref[...], ((1,), (1,))) * inverse).astype(BF16)
        total = mm(d_pre, self_ref[...], ((1,), (1,)))
        total = total + mm(high_ref[REACH], back, ((0,), (0,)))
        total_ref[:, cols] = total + mm(low_ref[REACH], back, ((0,), (0,)))


def later_kernel(
    local_confs,
    distance,
    scale,
    d_row_ref,
    total_ref,
    own_ref,
    near_a_ref,
    near_b_ref,
    far_a_ref,
    far_b_ref,
    note_ref,
    expand_ref,
    self_ref,
    neigh_ref,
    out_ref,
    bias_ref,
    result_ref,
):
    hid = self_ref.shape[0]
    nodes = total_ref.shape[0]
    slots = expand_ref.shape[0]
    step = nodes // local_confs
    note = note_ref[...]
    notes = note[WINDOW * step :, :nodes].astype(F32)
    segment = column_of(notes[0:1], slots).astype(jnp.int32)
    inverse = 1.0 / jnp.maximum(column_of(notes[1:2], nodes), 1.0)
    present = lax.axis_index("row") + distance < lax.axis_size("row")
    mask = (segment == iota((nodes, slots), 1) % SEGS).astype(F32) * present.astype(F32)
    factors = split_two(mask * d_row_ref[0:1, :])
    tiles = []
    for reach in range(WINDOW):
        rows = slice(reach * step, (reach + 1) * step)
        parts = [note[rows, part * nodes : (part + 1) * nodes] for part in range(local_confs)]
        tiles.append(jnp.concatenate(parts, axis=0))
    w_out = out_ref[...]
    for conf in range(local_confs):
        cols = slice(conf * hid, (conf + 1) * hid)
        before, after = panels(1, near_a_ref[:, cols], near_b_ref[:, cols])
        sources = [before, own_ref[:, cols], after]
        if distance == 2:
            sources = sources[1:] + [panels(2, far_a_ref[:, cols], far_b_ref[:, cols])[1]]
        summed = mm(tiles[0], sources[0]) + mm(tiles[1], sources[1]) + mm(tiles[2], sources[2])
        mean = (summed * inverse).astype(BF16)
        pre = mm(sources[2], self_ref[...]) + mm(mean, neigh_ref[...]) + bias_ref[...]
        sigm = sigmoid(pre)
        slope = w_out * (sigm * (1.0 + pre * (1.0 - sigm)))
        expand = expand_ref[:, cols]
        d_node = mm(factors[0], expand) + mm(factors[1], expand)
        d_pre = (d_node * slope).astype(BF16)
        back = (mm(d_pre, neigh_ref[...], ((1,), (1,))) * inverse).astype(BF16)
        total = total_ref[:, cols] + mm(tiles[REACH - distance], back, ((0,), (0,)))
        result_ref[:, cols] = (total * scale).astype(result_ref.dtype)


def final_kernel(main, count, *refs):
    hid = refs[0].shape[1]
    parts = [ref[...].astype(F32) for ref in refs[:count]]
    if count == 4:
        total = (parts[0] + parts[1]) + (parts[2] + parts[3])
    else:
        total = parts[0] + parts[1]
    self_ref, neigh_ref, bias_ref, out_ref = refs[count:]
    self_ref[...] = total[:hid]
    neigh_ref[...] = total[hid:main]
    extra = (total.shape[0] - main) // 3
    rows = [vectors(part, main, extra) for part in parts]
    if count == 4:
        row = (rows[0] + rows[1]) + (rows[2] + rows[3])
    else:
        row = rows[0] + rows[1]
    bias_ref[...] = row[0:1]
    out_ref[...] = row[1:2]


def vectors(message, main, extra):
    high, middle, last = (
        message[main + i * extra : main + (i + 1) * extra] for i in range(3)
    )
    return high + middle + last


def rounded(value):
    return lax.reduce_precision(value, 8, 7)


def packed(total, main):
    vectors = total[main:]
    high = rounded(vectors)
    middle = rounded(vectors - high)
    last = rounded(vectors - high - middle)
    return jnp.concatenate([rounded(total[:main]), high, middle, last], axis=0).astype(BF16)


def unpacked(message, main):
    message = message.astype(F32)
    extra = (message.shape[0] - main) // 3
    parts = [message[main + i * extra : main + (i + 1) * extra] for i in range(3)]
    return jnp.concatenate([message[:main], parts[0] + parts[1] + parts[2]], axis=0)


def row_stages(count):
    stride = 1
    while stride < count:
        yield [stride * k for k in (1, 2, 3) if stride * k < count]
        stride *= 4


def finished(parts, main, hid):
    outs = (shape((hid, hid), F32), shape((hid, hid), F32), shape((1, hid), F32), shape((1, hid), F32))
    return kernel_call(
        functools.partial(final_kernel, main, len(parts)), outs, [], "finish", 1 << 20, parts
    )


def four_summed(parts):
    return (parts[0] + parts[1]) + (parts[2] + parts[3])


def shape(dims, dtype):
    return jax.ShapeDtypeStruct(dims, dtype)


def kernel_call(kernel, outs, spaces, name, flops, operands, scratch=()):
    moved = sum(math.prod(leaf.shape) * leaf.dtype.itemsize for leaf in tuple(operands) + tuple(outs))
    spaces = list(spaces) + [pltpu.VMEM] * (len(operands) - len(spaces))
    return pl.pallas_call(
        kernel,
        out_shape=outs,
        in_specs=[pl.BlockSpec(memory_space=space) for space in spaces],
        out_specs=(pl.BlockSpec(memory_space=pltpu.VMEM),) * len(outs),
        scratch_shapes=scratch,
        compiler_params=pltpu.CompilerParams(vmem_limit_bytes=LIMIT),
        cost_estimate=pl.CostEstimate(flops=flops, bytes_accessed=moved, transcendentals=0),
        name=name,
    )(*operands)


def body(features, tiles, pattern, degrees, segments, pairs, w_self, w_neigh, bias, w_out):
    nodes, width = features.shape
    hid = w_self.shape[0]
    local_confs = width // hid
    rows, columns = lax.axis_size("row"), lax.axis_size("col")
    product = 2 * nodes * nodes * width
    slots = local_confs * columns * SEGS
    near_a, near_b, far_a, far_b = around(features)
    wide = shape((nodes, width), F32)
    narrow = shape((nodes, width), BF16)
    square = shape((nodes, nodes), F32)
    weight = shape((hid, hid), BF16)
    tile_set = shape((WINDOW, nodes, nodes), BF16)
    degree_row, segment_row = degrees.reshape(1, nodes), segments.reshape(1, nodes)
    in_hbm = [
        pltpu.with_memory_space_constraint(value, pltpu.HBM)
        for value in (features, tiles, w_self, w_neigh)
    ]
    own, high, low, payload = kernel_call(
        functools.partial(parcel_kernel, local_confs),
        (
            narrow,
            tile_set,
            tile_set,
            shape((WINDOW * (nodes // local_confs) + 8, width), BF16),
        ),
        [pltpu.SMEM] + [pltpu.HBM] * 2,
        "parcel",
        product,
        (pattern, in_hbm[0], in_hbm[1], degree_row, segment_row),
        (pltpu.VMEM(tiles.shape, tiles.dtype), pltpu.SemaphoreType.DMA((2,))),
    )
    (
        self_w,
        neigh_w,
        out_w,
        bias_w,
        base,
        summed,
        inverse,
        expand,
        mask,
        chosen,
        stub,
    ) = kernel_call(
        functools.partial(prepare_kernel, local_confs),
        (
            weight,
            weight,
            shape((1, hid), F32),
            shape((1, hid), F32),
            wide,
            wide,
            square,
            shape((slots, width), BF16),
            shape((nodes, slots), F32),
            shape((slots, pairs.shape[0]), BF16),
            shape((8, slots), F32),
        ),
        [pltpu.HBM] * 2,
        "prepare",
        3 * product,
        (
            in_hbm[2],
            in_hbm[3],
            own,
            high,
            low,
            degree_row,
            segment_row,
            pairs.T,
            bias.reshape(1, hid),
            w_out.reshape(1, hid),
        ),
        (pltpu.SemaphoreType.DMA((2,)),),
    )
    base, payload = lax.optimization_barrier((base, payload))
    one = shifted(payload, "row", -1)
    two = shifted(payload, "row", -2)
    notes = (one, two)
    mean, slope, hidden, message = kernel_call(
        functools.partial(forward_kernel, local_confs),
        (
            narrow,
            wide,
            shape((slots, hid), F32),
            shape((rows * columns, 8, slots), F32),
        ),
        [],
        "forward",
        6 * product,
        (near_a, near_b, far_a, far_b, neigh_w, out_w, high, low, base, summed, inverse, stub),
    )
    message, notes = lax.optimization_barrier((message, notes))
    received = lax.all_to_all(message, ("row", "col"), 0, 0, tiled=True)
    received, notes = lax.optimization_barrier((received, notes))
    main = 2 * hid
    grads, loss, d_pre, d_row = kernel_call(
        functools.partial(gradient_kernel, local_confs),
        (
            shape((main + 8, hid), F32),
            shape((1, 1), F32),
            narrow,
            shape((8, slots), F32),
        ),
        [],
        "gradient",
        3 * product,
        (received, chosen, mask, expand, own, mean, slope, hidden),
    )
    scale = math.sqrt(nodes * rows / SEGS)
    (node_total,) = kernel_call(
        functools.partial(own_kernel, local_confs),
        (wide,),
        [],
        "own",
        4 * product,
        (d_pre, self_w, neigh_w, inverse, high, low),
    )

    def later(distance, d_row, node_total, out, factor):
        (result,) = kernel_call(
            functools.partial(later_kernel, local_confs, distance, factor),
            (out,),
            [],
            f"later{distance}",
            10 * product,
            (
                d_row,
                node_total,
                own,
                near_a,
                near_b,
                far_a,
                far_b,
                notes[distance - 1],
                expand,
                self_w,
                neigh_w,
                out_w,
                bias_w,
            ),
        )
        return result

    total = grads
    for step in range(columns.bit_length() - 1):
        total = total + exchanged(total, "col", 1 << step)
    total, d_row, node_total = lax.optimization_barrier((total, d_row, node_total))
    node_total = later(1, d_row, node_total, wide, 1.0)
    stages = list(row_stages(rows))
    for index, stage in enumerate(stages):
        packet = packed(total, main)
        parts = [packet] + [exchanged(packet, "row", bits) for bits in stage]
        if index == len(stages) - 1:
            break
        total = [unpacked(part, main) for part in parts]
        total = four_summed(total) if len(total) == 4 else total[0] + total[1]
        if index == len(stages) - 2:
            total, d_row, node_total = lax.optimization_barrier((total, d_row, node_total))
    grad_self, grad_neigh, grad_bias, grad_out = finished(parts, main, hid)
    node_grad = later(2, d_row, node_total, narrow, scale)
    return (
        loss.reshape(1),
        grad_self,
        grad_neigh,
        grad_bias.reshape(hid),
        grad_out.reshape(hid),
        node_grad,
    )


def solution(mesh):
    in_specs = (
        P(("groups", "row"), "col"),
        P(("groups", "row"), None, None, None),
        P(("groups", "row"), None),
        P(("groups", "row")),
        P(("groups", "row")),
        P("groups", None),
        P(),
        P(),
        P(),
        P(),
    )
    out_specs = (
        P("groups"),
        P("groups", None),
        P("groups", None),
        P("groups"),
        P("groups"),
        P(("groups", "row"), "col"),
    )
    return jax.shard_map(body, mesh=mesh, in_specs=in_specs, out_specs=out_specs, check_vma=False)
```

```python
import functools
import math

import jax
import jax.numpy as jnp
from jax import lax
from jax.experimental import pallas as pl
from jax.experimental.pallas import tpu as pltpu
from jax.sharding import PartitionSpec as P

REACH = 2
SEGS = 8
WINDOW = REACH + 1
F32 = jnp.float32
BF16 = jnp.bfloat16
HIGHEST = lax.Precision.HIGHEST
VMEM = pl.BlockSpec(memory_space=pltpu.VMEM)
SMEM = pl.BlockSpec(memory_space=pltpu.SMEM)
LIMIT = 24 << 20


def paired(value, steps, phase):
    rows, groups = lax.axis_size("row"), lax.axis_size("groups")
    route = []
    for group in range(groups):
        for row in range(rows):
            target = row + steps if row // steps % 2 == phase else row - steps
            other = group
            if not 0 <= target < rows:
                target = row
                other = group ^ 1 if groups % 2 == 0 else group
            route.append((group * rows + row, other * rows + target))
    return lax.ppermute(value, ("groups", "row"), route)


def shifted(value, axis, steps):
    count = lax.axis_size(axis)
    initial, last = (max(0, -steps), min(count, count - steps))
    return lax.ppermute(value, axis, [(source, source + steps) for source in range(initial, last)])


def around(value):
    order = ((2, 0), (2, 1), (1, 1), (1, 0))
    found = {where: paired(value, *where) for where in order}
    return tuple(found[steps, phase] for steps in (1, 2) for phase in (0, 1))


def panels(steps, first, second):
    even = lax.axis_index("row") // steps % 2 == 0
    return jnp.where(even, second, first), jnp.where(even, first, second)


def exchanged(value, axis, bit):
    count = lax.axis_size(axis)
    return lax.ppermute(value, axis, [(source, source ^ bit) for source in range(count)])


def mm(left, right, contract=((1,), (0,))):
    return lax.dot_general(left, right, (contract, ((), ())), preferred_element_type=F32)


def mm_exact(left, right, contract):
    return lax.dot_general(
        left, right, (contract, ((), ())), precision=HIGHEST, preferred_element_type=F32
    )


def split_two(value):
    high = value.astype(BF16)
    return high, (value - high.astype(F32)).astype(BF16)


def split_three(value):
    high, rest = value.astype(BF16), value
    rest = rest - high.astype(F32)
    middle = rest.astype(BF16)
    return high, middle, (rest - middle.astype(F32)).astype(BF16)


def sigmoid(value):
    return 0.5 + 0.5 * jnp.tanh(0.5 * value)


def iota(dims, dim):
    return lax.broadcasted_iota(jnp.int32, dims, dim)


def column_of(row, count):
    return jnp.broadcast_to(row.astype(F32), (count, row.shape[1])).T


def parcel_kernel(
    local_confs,
    pattern_ref,
    features_ref,
    tiles_ref,
    degree_ref,
    segments_ref,
    own_ref,
    high_ref,
    low_ref,
    payload_ref,
    full_ref,
    tiles_buffer,
    sems,
):
    copies = [
        pltpu.make_async_copy(source, target, sems.at[i])
        for i, (source, target) in enumerate(((tiles_ref, tiles_buffer), (features_ref, own_ref)))
    ]
    for copy in copies:
        copy.start()
    nodes = own_ref.shape[0]
    lowest = lax.axis_index("row") - REACH
    step = nodes // local_confs
    segment_row = segments_ref[...]
    notes = jnp.where(iota((8, nodes), 0) == 0, segment_row, degree_ref[...])
    notes = notes.astype(F32).astype(BF16)
    full_ref[WINDOW * step :] = jnp.concatenate([notes] * local_confs, axis=1)
    copies[0].wait()
    for reach in range(WINDOW):
        total = None
        for index in range(tiles_buffer.shape[1]):
            keep = (pattern_ref[0, index] - lowest == reach).astype(F32)
            term = tiles_buffer[0, index].astype(F32) * keep
            total = term if total is None else total + term
        high, low = split_two(total)
        high_ref[reach] = high
        low_ref[reach] = low
        rows = slice(reach * step, (reach + 1) * step)
        for part in range(local_confs):
            full_ref[rows, part * nodes : (part + 1) * nodes] = high[
                part * step : (part + 1) * step
            ]
    share = payload_ref.shape[0]
    start = lax.axis_index("col") * (full_ref.shape[0] - share)
    payload_ref[...] = full_ref[pl.ds(pl.multiple_of(start, 8), share), :]
    copies[1].wait()


def prepare_kernel(
    local_confs,
    self_w_ref,
    neigh_w_ref,
    own_ref,
    high_ref,
    low_ref,
    degree_ref,
    segments_ref,
    pairs_ref,
    bias_ref,
    w_out_ref,
    self_ref,
    neigh_ref,
    out_ref,
    bias_out_ref,
    base_ref,
    summed_ref,
    inverse_ref,
    expand_ref,
    mask_ref,
    chosen_ref,
    stub_ref,
    sems,
):
    copies = [
        pltpu.make_async_copy(source, target, sems.at[i])
        for i, (source, target) in enumerate(((self_w_ref, self_ref), (neigh_w_ref, neigh_ref)))
    ]
    for copy in copies:
        copy.start()
    nodes, hid = own_ref.shape[0], self_ref.shape[0]
    first_conf = lax.axis_index("col") * local_confs
    out_ref[...] = w_out_ref[...]
    bias_out_ref[...] = bias_ref[...]
    inverse_ref[...] = 1.0 / column_of(degree_ref[...], nodes)
    slots = expand_ref.shape[0]
    for conf in range(local_confs):
        cols = slice(conf * hid, (conf + 1) * hid)
        chosen = iota((slots, hid), 0) // SEGS == first_conf + conf
        expand_ref[:, cols] = chosen.astype(F32).astype(BF16)
    segment_row = segments_ref[...]
    segment = column_of(segment_row, slots).astype(jnp.int32)
    mask = (segment == iota((nodes, slots), 1) % SEGS).astype(F32)
    mask_ref[...] = mask
    slot = iota((slots, pairs_ref.shape[1]), 0)
    segment = pairs_ref[0:1, :]
    first = (pairs_ref[1:2, :] * SEGS + segment == slot).astype(F32)
    second = (pairs_ref[2:3, :] * SEGS + segment == slot).astype(F32)
    chosen_ref[...] = (first - second).astype(BF16)
    counts = jnp.sum(mask, axis=0, keepdims=True) * (first_conf == 0).astype(F32)
    sub = iota((8, slots), 0)
    stub_ref[...] = jnp.where(sub == 1, counts, 0.0) + jnp.where(
        sub == 2, segment_row.astype(F32), 0.0
    )
    own = own_ref[...]
    summed_ref[...] = mm(high_ref[REACH], own) + mm(low_ref[REACH], own)
    copies[0].wait()
    for conf in range(local_confs):
        cols = slice(conf * hid, (conf + 1) * hid)
        base_ref[:, cols] = mm(own_ref[:, cols], self_ref[...]) + bias_ref[...]
    copies[1].wait()


def forward_kernel(
    local_confs,
    near_a_ref,
    near_b_ref,
    far_a_ref,
    far_b_ref,
    neigh_ref,
    out_ref,
    high_ref,
    low_ref,
    base_ref,
    summed_ref,
    inverse_ref,
    stub_ref,
    mean_ref,
    slope_ref,
    hidden_ref,
    message_ref,
):
    nodes, hid = base_ref.shape[0], neigh_ref.shape[0]
    summed = summed_ref[...]
    far = panels(2, far_a_ref[...], far_b_ref[...])[0]
    near = panels(1, near_a_ref[...], near_b_ref[...])[0]
    weights = [ref[reach] for reach in (0, 1) for ref in (high_ref, low_ref)]
    summed = summed + mm(
        jnp.concatenate(weights, axis=1), jnp.concatenate([far, far, near, near], axis=0)
    )
    inverse = inverse_ref[...]
    w_out = out_ref[...]
    segment_row = stub_ref[2:3, :].astype(jnp.int32)
    member = (segment_row == iota((SEGS, nodes), 0)).astype(F32).astype(BF16)
    first_conf = lax.axis_index("col") * local_confs
    member = jnp.concatenate([member, member], axis=1)
    hidden_ref[...] = jnp.zeros_like(hidden_ref)
    for conf in range(local_confs):
        cols = slice(conf * hid, (conf + 1) * hid)
        mean = (summed[:, cols] * inverse).astype(BF16)
        mean_ref[:, cols] = mean
        pre = base_ref[:, cols] + mm(mean, neigh_ref[...])
        sigm = sigmoid(pre)
        hidden = pre * sigm
        slope = w_out * (sigm * (1.0 + pre * (1.0 - sigm)))
        slope_ref[:, cols] = slope
        pair = jnp.concatenate(split_two(hidden), axis=0)
        start = pl.multiple_of((first_conf + conf) * SEGS, SEGS)
        hidden_ref[pl.ds(start, SEGS), :] = mm(member, pair)
    scores = mm_exact(jnp.broadcast_to(w_out, (8, hid)), hidden_ref[...], ((1,), (1,)))
    message = stub_ref[...] + jnp.where(iota(scores.shape, 0) == 0, scores, 0.0)
    for peer in range(message_ref.shape[0]):
        message_ref[peer] = message


def gradient_kernel(
    local_confs,
    received_ref,
    chosen_ref,
    mask_ref,
    expand_ref,
    own_ref,
    mean_ref,
    slope_ref,
    hidden_ref,
    grads_ref,
    loss_ref,
    d_pre_ref,
    d_row_ref,
):
    hid = grads_ref.shape[1]
    total = jnp.sum(received_ref[...], axis=0)
    root = jnp.sqrt(total[1:2])
    scores = total[0:1] / root
    chosen = chosen_ref[...]

    def one_row(row, contract):
        parts = jnp.concatenate([part.astype(F32) for part in split_three(row)], axis=0)
        parts = jnp.concatenate([parts, jnp.zeros((5, row.shape[1]), F32)], axis=0).astype(BF16)
        return jnp.sum(mm(parts, chosen, contract), axis=0, keepdims=True)

    margin = jnp.maximum(0.0, 1.0 - one_row(scores, ((1,), (0,))))
    loss_ref[...] = jnp.sum(margin * margin, axis=1, keepdims=True)
    d_row = one_row(-2.0 * margin, ((1,), (1,))) / root
    d_rows = jnp.broadcast_to(d_row, d_row_ref.shape)
    d_row_ref[...] = d_rows
    factors = split_three(mask_ref[...] * d_row)
    grads = None
    d_bias = None
    for conf in range(local_confs):
        cols = slice(conf * hid, (conf + 1) * hid)
        expand = expand_ref[:, cols]
        d_node = mm(factors[0], expand) + mm(factors[1], expand) + mm(factors[2], expand)
        d_pre = d_node * slope_ref[:, cols]
        d_pre_b = d_pre.astype(BF16)
        d_pre_ref[:, cols] = d_pre_b
        rows = jnp.concatenate([own_ref[:, cols], mean_ref[:, cols]], axis=1)
        term = mm(rows, d_pre_b, ((0,), (0,)))
        grads = term if grads is None else grads + term
        d_bias = d_pre if d_bias is None else d_bias + d_pre
    grads_ref[: 2 * hid] = grads
    d_out = mm_exact(d_rows, hidden_ref[...], ((1,), (0,)))
    d_bias = jnp.sum(d_bias, axis=0, keepdims=True)
    sub = iota((8, hid), 0)
    grads_ref[2 * hid :] = jnp.where(sub == 0, d_bias, 0.0) + jnp.where(sub == 1, d_out, 0.0)


def own_kernel(
    local_confs,
    d_pre_ref,
    self_ref,
    neigh_ref,
    inverse_ref,
    high_ref,
    low_ref,
    total_ref,
):
    hid = self_ref.shape[0]
    inverse = inverse_ref[...]
    for conf in range(local_confs):
        cols = slice(conf * hid, (conf + 1) * hid)
        d_pre = d_pre_ref[:, cols]
        back = (mm(d_pre, neigh_ref[...], ((1,), (1,))) * inverse).astype(BF16)
        total = mm(d_pre, self_ref[...], ((1,), (1,)))
        total = total + mm(high_ref[REACH], back, ((0,), (0,)))
        total_ref[:, cols] = total + mm(low_ref[REACH], back, ((0,), (0,)))


def later_kernel(
    local_confs,
    distance,
    scale,
    d_row_ref,
    total_ref,
    own_ref,
    near_a_ref,
    near_b_ref,
    far_a_ref,
    far_b_ref,
    note_ref,
    note_other_ref,
    expand_ref,
    self_ref,
    neigh_ref,
    out_ref,
    bias_ref,
    result_ref,
):
    hid = self_ref.shape[0]
    nodes = total_ref.shape[0]
    slots = expand_ref.shape[0]
    step = nodes // local_confs
    first_core = lax.axis_index("col") == 0
    upper = jnp.where(first_core, note_ref[...], note_other_ref[...])
    lower = jnp.where(first_core, note_other_ref[...], note_ref[...])
    share = upper.shape[0]
    note = jnp.concatenate([upper, lower[2 * share - WINDOW * step - 8 :]], axis=0)
    notes = note[WINDOW * step :, :nodes].astype(F32)
    segment = column_of(notes[0:1], slots).astype(jnp.int32)
    inverse = 1.0 / jnp.maximum(column_of(notes[1:2], nodes), 1.0)
    present = lax.axis_index("row") + distance < lax.axis_size("row")
    mask = (segment == iota((nodes, slots), 1) % SEGS).astype(F32) * present.astype(F32)
    factors = split_two(mask * d_row_ref[0:1, :])
    tiles = []
    for reach in range(WINDOW):
        rows = slice(reach * step, (reach + 1) * step)
        parts = [note[rows, part * nodes : (part + 1) * nodes] for part in range(local_confs)]
        tiles.append(jnp.concatenate(parts, axis=0))
    weights = jnp.concatenate([self_ref[...], neigh_ref[...]], axis=0)
    w_out = out_ref[...]
    for conf in range(local_confs):
        cols = slice(conf * hid, (conf + 1) * hid)
        before, after = panels(1, near_a_ref[:, cols], near_b_ref[:, cols])
        sources = [before, own_ref[:, cols], after]
        if distance == 2:
            sources = sources[1:] + [panels(2, far_a_ref[:, cols], far_b_ref[:, cols])[1]]
        summed = mm(tiles[0], sources[0]) + mm(tiles[1], sources[1]) + mm(tiles[2], sources[2])
        mean = (summed * inverse).astype(BF16)
        pre = mm(jnp.concatenate([sources[2], mean], axis=1), weights) + bias_ref[...]
        sigm = sigmoid(pre)
        slope = w_out * (sigm * (1.0 + pre * (1.0 - sigm)))
        expand = expand_ref[:, cols]
        d_node = mm(factors[0], expand) + mm(factors[1], expand)
        d_pre = (d_node * slope).astype(BF16)
        back = (mm(d_pre, neigh_ref[...], ((1,), (1,))) * inverse).astype(BF16)
        total = total_ref[:, cols] + mm(tiles[REACH - distance], back, ((0,), (0,)))
        result_ref[:, cols] = (total * scale).astype(result_ref.dtype)


def final_kernel(main, count, *refs):
    hid = refs[0].shape[1]
    parts = [ref[...].astype(F32) for ref in refs[:count]]
    if count == 4:
        total = (parts[0] + parts[1]) + (parts[2] + parts[3])
    else:
        total = parts[0] + parts[1]
    self_ref, neigh_ref, bias_ref, out_ref = refs[count:]
    self_ref[...] = total[:hid]
    neigh_ref[...] = total[hid:main]
    extra = (total.shape[0] - main) // 3
    rows = [vectors(part, main, extra) for part in parts]
    if count == 4:
        row = (rows[0] + rows[1]) + (rows[2] + rows[3])
    else:
        row = rows[0] + rows[1]
    bias_ref[...] = row[0:1]
    out_ref[...] = row[1:2]


def vectors(message, main, extra):
    high, middle, last = (
        message[main + i * extra : main + (i + 1) * extra] for i in range(3)
    )
    return high + middle + last


def rounded(value):
    return lax.reduce_precision(value, 8, 7)


def packed(total, main):
    vectors = total[main:]
    high = rounded(vectors)
    middle = rounded(vectors - high)
    last = rounded(vectors - high - middle)
    return jnp.concatenate([rounded(total[:main]), high, middle, last], axis=0).astype(BF16)


def unpacked(message, main):
    message = message.astype(F32)
    extra = (message.shape[0] - main) // 3
    parts = [message[main + i * extra : main + (i + 1) * extra] for i in range(3)]
    return jnp.concatenate([message[:main], parts[0] + parts[1] + parts[2]], axis=0)


def row_stages(count):
    stride = 1
    while stride < count:
        yield [stride * k for k in (1, 2, 3) if stride * k < count]
        stride *= 4


def finished(parts, main, hid):
    outs = (shape((hid, hid), F32), shape((hid, hid), F32), shape((1, hid), F32), shape((1, hid), F32))
    return kernel_call(
        functools.partial(final_kernel, main, len(parts)), outs, [], "finish", 1 << 20, parts
    )


def four_summed(parts):
    return (parts[0] + parts[1]) + (parts[2] + parts[3])


def shape(dims, dtype):
    return jax.ShapeDtypeStruct(dims, dtype)


def kernel_call(kernel, outs, spaces, name, flops, operands, scratch=()):
    moved = sum(math.prod(leaf.shape) * leaf.dtype.itemsize for leaf in tuple(operands) + tuple(outs))
    spaces = list(spaces) + [pltpu.VMEM] * (len(operands) - len(spaces))
    return pl.pallas_call(
        kernel,
        out_shape=outs,
        in_specs=[pl.BlockSpec(memory_space=space) for space in spaces],
        out_specs=(pl.BlockSpec(memory_space=pltpu.VMEM),) * len(outs),
        scratch_shapes=scratch,
        compiler_params=pltpu.CompilerParams(vmem_limit_bytes=LIMIT),
        cost_estimate=pl.CostEstimate(flops=flops, bytes_accessed=moved, transcendentals=0),
        name=name,
    )(*operands)


def body(features, tiles, pattern, degrees, segments, pairs, w_self, w_neigh, bias, w_out):
    nodes, width = features.shape
    hid = w_self.shape[0]
    local_confs = width // hid
    rows, columns = lax.axis_size("row"), lax.axis_size("col")
    product = 2 * nodes * nodes * width
    slots = local_confs * columns * SEGS
    near_a, near_b, far_a, far_b = around(features)
    wide = shape((nodes, width), F32)
    narrow = shape((nodes, width), BF16)
    square = shape((nodes, nodes), F32)
    weight = shape((hid, hid), BF16)
    tile_set = shape((WINDOW, nodes, nodes), BF16)
    degree_row, segment_row = degrees.reshape(1, nodes), segments.reshape(1, nodes)
    in_hbm = [
        pltpu.with_memory_space_constraint(value, pltpu.HBM)
        for value in (features, tiles, w_self, w_neigh)
    ]
    note_rows = WINDOW * (nodes // local_confs) + 8
    share = -(-note_rows // 16) * 8 if columns == 2 else note_rows
    own, high, low, payload = kernel_call(
        functools.partial(parcel_kernel, local_confs),
        (
            narrow,
            tile_set,
            tile_set,
            shape((share, width), BF16),
        ),
        [pltpu.SMEM] + [pltpu.HBM] * 2,
        "parcel",
        product,
        (pattern, in_hbm[0], in_hbm[1], degree_row, segment_row),
        (
            pltpu.VMEM((note_rows, width), BF16),
            pltpu.VMEM(tiles.shape, tiles.dtype),
            pltpu.SemaphoreType.DMA((2,)),
        ),
    )
    (
        self_w,
        neigh_w,
        out_w,
        bias_w,
        base,
        summed,
        inverse,
        expand,
        mask,
        chosen,
        stub,
    ) = kernel_call(
        functools.partial(prepare_kernel, local_confs),
        (
            weight,
            weight,
            shape((1, hid), F32),
            shape((1, hid), F32),
            wide,
            wide,
            square,
            shape((slots, width), BF16),
            shape((nodes, slots), F32),
            shape((slots, pairs.shape[0]), BF16),
            shape((8, slots), F32),
        ),
        [pltpu.HBM] * 2,
        "prepare",
        3 * product,
        (
            in_hbm[2],
            in_hbm[3],
            own,
            high,
            low,
            degree_row,
            segment_row,
            pairs.T,
            bias.reshape(1, hid),
            w_out.reshape(1, hid),
        ),
        (pltpu.SemaphoreType.DMA((2,)),),
    )
    base, payload = lax.optimization_barrier((base, payload))
    one = shifted(payload, "row", -1)
    two = shifted(payload, "row", -2)
    notes = (one, two)
    mean, slope, hidden, message = kernel_call(
        functools.partial(forward_kernel, local_confs),
        (
            narrow,
            wide,
            shape((slots, hid), F32),
            shape((rows * columns, 8, slots), F32),
        ),
        [],
        "forward",
        6 * product,
        (near_a, near_b, far_a, far_b, neigh_w, out_w, high, low, base, summed, inverse, stub),
    )
    message, notes = lax.optimization_barrier((message, notes))
    received = lax.all_to_all(message, ("row", "col"), 0, 0, tiled=True)
    received, notes = lax.optimization_barrier((received, notes))
    if columns == 2:
        received, notes = lax.optimization_barrier((received, notes))
        notes = tuple((note, exchanged(note, "col", 1)) for note in notes)
    else:
        notes = tuple((note, note) for note in notes)
    main = 2 * hid
    grads, loss, d_pre, d_row = kernel_call(
        functools.partial(gradient_kernel, local_confs),
        (
            shape((main + 8, hid), F32),
            shape((1, 1), F32),
            narrow,
            shape((8, slots), F32),
        ),
        [],
        "gradient",
        3 * product,
        (received, chosen, mask, expand, own, mean, slope, hidden),
    )
    scale = math.sqrt(nodes * rows / SEGS)
    (node_total,) = kernel_call(
        functools.partial(own_kernel, local_confs),
        (wide,),
        [],
        "own",
        4 * product,
        (d_pre, self_w, neigh_w, inverse, high, low),
    )

    def later(distance, d_row, node_total, out, factor):
        (result,) = kernel_call(
            functools.partial(later_kernel, local_confs, distance, factor),
            (out,),
            [],
            f"later{distance}",
            10 * product,
            (
                d_row,
                node_total,
                own,
                near_a,
                near_b,
                far_a,
                far_b,
                *notes[distance - 1],
                expand,
                self_w,
                neigh_w,
                out_w,
                bias_w,
            ),
        )
        return result

    total = grads
    for step in range(columns.bit_length() - 1):
        total = total + exchanged(total, "col", 1 << step)
    total, d_row, node_total = lax.optimization_barrier((total, d_row, node_total))
    node_total = later(1, d_row, node_total, wide, 1.0)
    stages = list(row_stages(rows))
    for index, stage in enumerate(stages):
        packet = packed(total, main)
        parts = [packet] + [exchanged(packet, "row", bits) for bits in stage]
        if index == len(stages) - 1:
            break
        total = [unpacked(part, main) for part in parts]
        total = four_summed(total) if len(total) == 4 else total[0] + total[1]
        if index == len(stages) - 2:
            total, d_row, node_total = lax.optimization_barrier((total, d_row, node_total))
    grad_self, grad_neigh, grad_bias, grad_out = finished(parts, main, hid)
    node_grad = later(2, d_row, node_total, narrow, scale)
    return (
        loss.reshape(1),
        grad_self,
        grad_neigh,
        grad_bias.reshape(hid),
        grad_out.reshape(hid),
        node_grad,
    )


def solution(mesh):
    in_specs = (
        P(("groups", "row"), "col"),
        P(("groups", "row"), None, None, None),
        P(("groups", "row"), None),
        P(("groups", "row")),
        P(("groups", "row")),
        P("groups", None),
        P(),
        P(),
        P(),
        P(),
    )
    out_specs = (
        P("groups"),
        P("groups", None),
        P("groups", None),
        P("groups"),
        P("groups"),
        P(("groups", "row"), "col"),
    )
    return jax.shard_map(body, mesh=mesh, in_specs=in_specs, out_specs=out_specs, check_vma=False)
```

```python
import functools
import math

import jax
import jax.numpy as jnp
from jax import lax
from jax.experimental import pallas as pl
from jax.experimental.pallas import tpu as pltpu
from jax.sharding import PartitionSpec as P

REACH = 2
SEGS = 8
WINDOW = REACH + 1
F32 = jnp.float32
BF16 = jnp.bfloat16
HIGHEST = lax.Precision.HIGHEST
VMEM = pl.BlockSpec(memory_space=pltpu.VMEM)
SMEM = pl.BlockSpec(memory_space=pltpu.SMEM)
LIMIT = 24 << 20


def paired(value, steps, phase):
    rows, groups = lax.axis_size("row"), lax.axis_size("groups")
    route = []
    for group in range(groups):
        for row in range(rows):
            target = row + steps if row // steps % 2 == phase else row - steps
            other = group
            if not 0 <= target < rows:
                target = row
                other = group ^ 1 if groups % 2 == 0 else group
            route.append((group * rows + row, other * rows + target))
    return lax.ppermute(value, ("groups", "row"), route)


def shifted(value, axis, steps):
    count = lax.axis_size(axis)
    initial, last = (max(0, -steps), min(count, count - steps))
    return lax.ppermute(value, axis, [(source, source + steps) for source in range(initial, last)])


def around(value):
    order = ((2, 0), (2, 1), (1, 1), (1, 0))
    found = {where: paired(value, *where) for where in order}
    return tuple(found[steps, phase] for steps in (1, 2) for phase in (0, 1))


def panels(steps, first, second):
    even = lax.axis_index("row") // steps % 2 == 0
    return jnp.where(even, second, first), jnp.where(even, first, second)


def exchanged(value, axis, bit):
    count = lax.axis_size(axis)
    return lax.ppermute(value, axis, [(source, source ^ bit) for source in range(count)])


def mm(left, right, contract=((1,), (0,))):
    return lax.dot_general(left, right, (contract, ((), ())), preferred_element_type=F32)


def mm_exact(left, right, contract):
    return lax.dot_general(
        left, right, (contract, ((), ())), precision=HIGHEST, preferred_element_type=F32
    )


def split_two(value):
    high = value.astype(BF16)
    return high, (value - high.astype(F32)).astype(BF16)


def split_three(value):
    high, rest = value.astype(BF16), value
    rest = rest - high.astype(F32)
    middle = rest.astype(BF16)
    return high, middle, (rest - middle.astype(F32)).astype(BF16)


def sigmoid(value):
    return 0.5 + 0.5 * jnp.tanh(0.5 * value)


def iota(dims, dim):
    return lax.broadcasted_iota(jnp.int32, dims, dim)


def column_of(row, count):
    return jnp.broadcast_to(row.astype(F32), (count, row.shape[1])).T


def parcel_kernel(
    local_confs,
    pattern_ref,
    features_ref,
    tiles_ref,
    degree_ref,
    segments_ref,
    own_ref,
    high_ref,
    low_ref,
    payload_ref,
    full_ref,
    tiles_buffer,
    sems,
):
    copies = [
        pltpu.make_async_copy(source, target, sems.at[i])
        for i, (source, target) in enumerate(((tiles_ref, tiles_buffer), (features_ref, own_ref)))
    ]
    for copy in copies:
        copy.start()
    nodes = own_ref.shape[0]
    lowest = lax.axis_index("row") - REACH
    step = nodes // local_confs
    segment_row = segments_ref[...]
    notes = jnp.where(iota((8, nodes), 0) == 0, segment_row, degree_ref[...])
    notes = notes.astype(F32).astype(BF16)
    full_ref[WINDOW * step :] = jnp.concatenate([notes] * local_confs, axis=1)
    copies[0].wait()
    for reach in range(WINDOW):
        total = None
        for index in range(tiles_buffer.shape[1]):
            keep = (pattern_ref[0, index] - lowest == reach).astype(F32)
            term = tiles_buffer[0, index].astype(F32) * keep
            total = term if total is None else total + term
        high, low = split_two(total)
        high_ref[reach] = high
        low_ref[reach] = low
        rows = slice(reach * step, (reach + 1) * step)
        for part in range(local_confs):
            full_ref[rows, part * nodes : (part + 1) * nodes] = high[
                part * step : (part + 1) * step
            ]
    share = payload_ref.shape[0]
    start = lax.axis_index("col") * (full_ref.shape[0] - share)
    payload_ref[...] = full_ref[pl.ds(pl.multiple_of(start, 8), share), :]
    copies[1].wait()


def prepare_kernel(
    local_confs,
    self_w_ref,
    neigh_w_ref,
    own_ref,
    high_ref,
    low_ref,
    degree_ref,
    segments_ref,
    pairs_ref,
    bias_ref,
    w_out_ref,
    self_ref,
    neigh_ref,
    out_ref,
    bias_out_ref,
    base_ref,
    summed_ref,
    inverse_ref,
    expand_ref,
    mask_ref,
    chosen_ref,
    stub_ref,
    sems,
):
    copies = [
        pltpu.make_async_copy(source, target, sems.at[i])
        for i, (source, target) in enumerate(((self_w_ref, self_ref), (neigh_w_ref, neigh_ref)))
    ]
    for copy in copies:
        copy.start()
    nodes, hid = own_ref.shape[0], self_ref.shape[0]
    first_conf = lax.axis_index("col") * local_confs
    out_ref[...] = w_out_ref[...]
    bias_out_ref[...] = bias_ref[...]
    inverse_ref[...] = 1.0 / column_of(degree_ref[...], nodes)
    slots = expand_ref.shape[0]
    for conf in range(local_confs):
        cols = slice(conf * hid, (conf + 1) * hid)
        chosen = iota((slots, hid), 0) // SEGS == first_conf + conf
        expand_ref[:, cols] = chosen.astype(F32).astype(BF16)
    segment_row = segments_ref[...]
    segment = column_of(segment_row, slots).astype(jnp.int32)
    mask = (segment == iota((nodes, slots), 1) % SEGS).astype(F32)
    mask_ref[...] = mask
    slot = iota((slots, pairs_ref.shape[1]), 0)
    segment = pairs_ref[0:1, :]
    first = (pairs_ref[1:2, :] * SEGS + segment == slot).astype(F32)
    second = (pairs_ref[2:3, :] * SEGS + segment == slot).astype(F32)
    chosen_ref[...] = (first - second).astype(BF16)
    counts = jnp.sum(mask, axis=0, keepdims=True) * (first_conf == 0).astype(F32)
    sub = iota((8, slots), 0)
    stub_ref[...] = jnp.where(sub == 1, counts, 0.0) + jnp.where(
        sub == 2, segment_row.astype(F32), 0.0
    )
    own = own_ref[...]
    summed_ref[...] = mm(high_ref[REACH], own) + mm(low_ref[REACH], own)
    copies[0].wait()
    for conf in range(local_confs):
        cols = slice(conf * hid, (conf + 1) * hid)
        base_ref[:, cols] = mm(own_ref[:, cols], self_ref[...]) + bias_ref[...]
    copies[1].wait()


def forward_kernel(
    local_confs,
    near_a_ref,
    near_b_ref,
    far_a_ref,
    far_b_ref,
    neigh_ref,
    out_ref,
    high_ref,
    low_ref,
    base_ref,
    summed_ref,
    inverse_ref,
    stub_ref,
    mean_ref,
    slope_ref,
    hidden_ref,
    message_ref,
):
    nodes, hid = base_ref.shape[0], neigh_ref.shape[0]
    summed = summed_ref[...]
    far = panels(2, far_a_ref[...], far_b_ref[...])[0]
    near = panels(1, near_a_ref[...], near_b_ref[...])[0]
    weights = [ref[reach] for reach in (0, 1) for ref in (high_ref, low_ref)]
    summed = summed + mm(
        jnp.concatenate(weights, axis=1), jnp.concatenate([far, far, near, near], axis=0)
    )
    inverse = inverse_ref[...]
    w_out = out_ref[...]
    segment_row = stub_ref[2:3, :].astype(jnp.int32)
    member = (segment_row == iota((SEGS, nodes), 0)).astype(F32).astype(BF16)
    first_conf = lax.axis_index("col") * local_confs
    member = jnp.concatenate([member, member], axis=1)
    hidden_ref[...] = jnp.zeros_like(hidden_ref)
    for conf in range(local_confs):
        cols = slice(conf * hid, (conf + 1) * hid)
        mean = (summed[:, cols] * inverse).astype(BF16)
        mean_ref[:, cols] = mean
        pre = base_ref[:, cols] + mm(mean, neigh_ref[...])
        sigm = sigmoid(pre)
        hidden = pre * sigm
        slope = w_out * (sigm * (1.0 + pre * (1.0 - sigm)))
        slope_ref[:, cols] = slope
        pair = jnp.concatenate(split_two(hidden), axis=0)
        start = pl.multiple_of((first_conf + conf) * SEGS, SEGS)
        hidden_ref[pl.ds(start, SEGS), :] = mm(member, pair)
    scores = mm_exact(jnp.broadcast_to(w_out, (8, hid)), hidden_ref[...], ((1,), (1,)))
    message = stub_ref[...] + jnp.where(iota(scores.shape, 0) == 0, scores, 0.0)
    for peer in range(message_ref.shape[0]):
        message_ref[peer] = message


def gradient_kernel(
    local_confs,
    received_ref,
    chosen_ref,
    mask_ref,
    expand_ref,
    own_ref,
    mean_ref,
    slope_ref,
    hidden_ref,
    grads_ref,
    loss_ref,
    d_pre_ref,
    d_row_ref,
):
    hid = grads_ref.shape[1]
    total = jnp.sum(received_ref[...], axis=0)
    root = jnp.sqrt(total[1:2])
    scores = total[0:1] / root
    chosen = chosen_ref[...]

    def one_row(row, contract):
        parts = jnp.concatenate([part.astype(F32) for part in split_three(row)], axis=0)
        parts = jnp.concatenate([parts, jnp.zeros((5, row.shape[1]), F32)], axis=0).astype(BF16)
        return jnp.sum(mm(parts, chosen, contract), axis=0, keepdims=True)

    margin = jnp.maximum(0.0, 1.0 - one_row(scores, ((1,), (0,))))
    loss_ref[...] = jnp.sum(margin * margin, axis=1, keepdims=True)
    d_row = one_row(-2.0 * margin, ((1,), (1,))) / root
    d_rows = jnp.broadcast_to(d_row, d_row_ref.shape)
    d_row_ref[...] = d_rows
    factors = split_three(mask_ref[...] * d_row)
    grads = None
    d_bias = None
    for conf in range(local_confs):
        cols = slice(conf * hid, (conf + 1) * hid)
        expand = expand_ref[:, cols]
        d_node = mm(factors[0], expand) + mm(factors[1], expand) + mm(factors[2], expand)
        d_pre = d_node * slope_ref[:, cols]
        d_pre_b = d_pre.astype(BF16)
        d_pre_ref[:, cols] = d_pre_b
        rows = jnp.concatenate([own_ref[:, cols], mean_ref[:, cols]], axis=1)
        term = mm(rows, d_pre_b, ((0,), (0,)))
        grads = term if grads is None else grads + term
        d_bias = d_pre if d_bias is None else d_bias + d_pre
    grads_ref[: 2 * hid] = grads
    d_out = mm_exact(d_rows, hidden_ref[...], ((1,), (0,)))
    d_bias = jnp.sum(d_bias, axis=0, keepdims=True)
    sub = iota((8, hid), 0)
    grads_ref[2 * hid :] = jnp.where(sub == 0, d_bias, 0.0) + jnp.where(sub == 1, d_out, 0.0)


def own_kernel(
    local_confs,
    d_pre_ref,
    self_ref,
    neigh_ref,
    inverse_ref,
    high_ref,
    low_ref,
    total_ref,
):
    hid = self_ref.shape[0]
    inverse = inverse_ref[...]
    for conf in range(local_confs):
        cols = slice(conf * hid, (conf + 1) * hid)
        d_pre = d_pre_ref[:, cols]
        back = (mm(d_pre, neigh_ref[...], ((1,), (1,))) * inverse).astype(BF16)
        total = mm(d_pre, self_ref[...], ((1,), (1,)))
        total = total + mm(high_ref[REACH], back, ((0,), (0,)))
        total_ref[:, cols] = total + mm(low_ref[REACH], back, ((0,), (0,)))


def later_kernel(
    local_confs,
    distance,
    scale,
    d_row_ref,
    total_ref,
    own_ref,
    near_a_ref,
    near_b_ref,
    far_a_ref,
    far_b_ref,
    note_ref,
    note_other_ref,
    expand_ref,
    self_ref,
    neigh_ref,
    out_ref,
    bias_ref,
    result_ref,
):
    hid = self_ref.shape[0]
    nodes = total_ref.shape[0]
    slots = expand_ref.shape[0]
    step = nodes // local_confs
    first_core = lax.axis_index("col") == 0
    upper = jnp.where(first_core, note_ref[...], note_other_ref[...])
    lower = jnp.where(first_core, note_other_ref[...], note_ref[...])
    share = upper.shape[0]
    note = jnp.concatenate([upper, lower[2 * share - WINDOW * step - 8 :]], axis=0)
    notes = note[WINDOW * step :, :nodes].astype(F32)
    segment = column_of(notes[0:1], slots).astype(jnp.int32)
    inverse = 1.0 / jnp.maximum(column_of(notes[1:2], nodes), 1.0)
    present = lax.axis_index("row") + distance < lax.axis_size("row")
    mask = (segment == iota((nodes, slots), 1) % SEGS).astype(F32) * present.astype(F32)
    factors = split_two(mask * d_row_ref[0:1, :])
    tiles = []
    for reach in range(WINDOW):
        rows = slice(reach * step, (reach + 1) * step)
        parts = [note[rows, part * nodes : (part + 1) * nodes] for part in range(local_confs)]
        tiles.append(jnp.concatenate(parts, axis=0))
    weights = jnp.concatenate([self_ref[...], neigh_ref[...]], axis=0)
    w_out = out_ref[...]
    for conf in range(local_confs):
        cols = slice(conf * hid, (conf + 1) * hid)
        before, after = panels(1, near_a_ref[:, cols], near_b_ref[:, cols])
        sources = [before, own_ref[:, cols], after]
        if distance == 2:
            sources = sources[1:] + [panels(2, far_a_ref[:, cols], far_b_ref[:, cols])[1]]
        summed = mm(tiles[0], sources[0]) + mm(tiles[1], sources[1]) + mm(tiles[2], sources[2])
        mean = (summed * inverse).astype(BF16)
        pre = mm(jnp.concatenate([sources[2], mean], axis=1), weights) + bias_ref[...]
        sigm = sigmoid(pre)
        slope = w_out * (sigm * (1.0 + pre * (1.0 - sigm)))
        expand = expand_ref[:, cols]
        d_node = mm(factors[0], expand) + mm(factors[1], expand)
        d_pre = (d_node * slope).astype(BF16)
        back = (mm(d_pre, neigh_ref[...], ((1,), (1,))) * inverse).astype(BF16)
        total = total_ref[:, cols] + mm(tiles[REACH - distance], back, ((0,), (0,)))
        result_ref[:, cols] = (total * scale).astype(result_ref.dtype)


def final_kernel(main, count, *refs):
    hid = refs[0].shape[1]
    parts = [ref[...].astype(F32) for ref in refs[:count]]
    if count == 4:
        total = (parts[0] + parts[1]) + (parts[2] + parts[3])
    else:
        total = parts[0] + parts[1]
    self_ref, neigh_ref, bias_ref, out_ref = refs[count:]
    self_ref[...] = total[:hid]
    neigh_ref[...] = total[hid:main]
    extra = (total.shape[0] - main) // 3
    rows = [vectors(part, main, extra) for part in parts]
    if count == 4:
        row = (rows[0] + rows[1]) + (rows[2] + rows[3])
    else:
        row = rows[0] + rows[1]
    bias_ref[...] = row[0:1]
    out_ref[...] = row[1:2]


def vectors(message, main, extra):
    high, middle, last = (
        message[main + i * extra : main + (i + 1) * extra] for i in range(3)
    )
    return high + middle + last


def rounded(value):
    return lax.reduce_precision(value, 8, 7)


def packed(total, main):
    vectors = total[main:]
    high = rounded(vectors)
    middle = rounded(vectors - high)
    last = rounded(vectors - high - middle)
    return jnp.concatenate([rounded(total[:main]), high, middle, last], axis=0).astype(BF16)


def unpacked(message, main):
    message = message.astype(F32)
    extra = (message.shape[0] - main) // 3
    parts = [message[main + i * extra : main + (i + 1) * extra] for i in range(3)]
    return jnp.concatenate([message[:main], parts[0] + parts[1] + parts[2]], axis=0)


def row_stages(count):
    stride = 1
    while stride < count:
        yield [stride * k for k in (1, 2, 3) if stride * k < count]
        stride *= 4


def finished(parts, main, hid):
    outs = (shape((hid, hid), F32), shape((hid, hid), F32), shape((1, hid), F32), shape((1, hid), F32))
    return kernel_call(
        functools.partial(final_kernel, main, len(parts)), outs, [], "finish", 1 << 20, parts
    )


def four_summed(parts):
    return (parts[0] + parts[1]) + (parts[2] + parts[3])


def shape(dims, dtype):
    return jax.ShapeDtypeStruct(dims, dtype)


def kernel_call(kernel, outs, spaces, name, flops, operands, scratch=()):
    moved = sum(math.prod(leaf.shape) * leaf.dtype.itemsize for leaf in tuple(operands) + tuple(outs))
    spaces = list(spaces) + [pltpu.VMEM] * (len(operands) - len(spaces))
    return pl.pallas_call(
        kernel,
        out_shape=outs,
        in_specs=[pl.BlockSpec(memory_space=space) for space in spaces],
        out_specs=(pl.BlockSpec(memory_space=pltpu.VMEM),) * len(outs),
        scratch_shapes=scratch,
        compiler_params=pltpu.CompilerParams(vmem_limit_bytes=LIMIT),
        cost_estimate=pl.CostEstimate(flops=flops, bytes_accessed=moved, transcendentals=0),
        name=name,
    )(*operands)


def body(features, tiles, pattern, degrees, segments, pairs, w_self, w_neigh, bias, w_out):
    nodes, width = features.shape
    hid = w_self.shape[0]
    local_confs = width // hid
    rows, columns = lax.axis_size("row"), lax.axis_size("col")
    product = 2 * nodes * nodes * width
    slots = local_confs * columns * SEGS
    near_a, near_b, far_a, far_b = around(features)
    wide = shape((nodes, width), F32)
    narrow = shape((nodes, width), BF16)
    square = shape((nodes, nodes), F32)
    weight = shape((hid, hid), BF16)
    tile_set = shape((WINDOW, nodes, nodes), BF16)
    degree_row, segment_row = degrees.reshape(1, nodes), segments.reshape(1, nodes)
    in_hbm = [
        pltpu.with_memory_space_constraint(value, pltpu.HBM)
        for value in (features, tiles, w_self, w_neigh)
    ]
    note_rows = WINDOW * (nodes // local_confs) + 8
    share = -(-note_rows // 16) * 8 if columns == 2 else note_rows
    own, high, low, payload = kernel_call(
        functools.partial(parcel_kernel, local_confs),
        (
            narrow,
            tile_set,
            tile_set,
            shape((share, width), BF16),
        ),
        [pltpu.SMEM] + [pltpu.HBM] * 2,
        "parcel",
        product,
        (pattern, in_hbm[0], in_hbm[1], degree_row, segment_row),
        (
            pltpu.VMEM((note_rows, width), BF16),
            pltpu.VMEM(tiles.shape, tiles.dtype),
            pltpu.SemaphoreType.DMA((2,)),
        ),
    )
    (
        self_w,
        neigh_w,
        out_w,
        bias_w,
        base,
        summed,
        inverse,
        expand,
        mask,
        chosen,
        stub,
    ) = kernel_call(
        functools.partial(prepare_kernel, local_confs),
        (
            weight,
            weight,
            shape((1, hid), F32),
            shape((1, hid), F32),
            wide,
            wide,
            square,
            shape((slots, width), BF16),
            shape((nodes, slots), F32),
            shape((slots, pairs.shape[0]), BF16),
            shape((8, slots), F32),
        ),
        [pltpu.HBM] * 2,
        "prepare",
        3 * product,
        (
            in_hbm[2],
            in_hbm[3],
            own,
            high,
            low,
            degree_row,
            segment_row,
            pairs.T,
            bias.reshape(1, hid),
            w_out.reshape(1, hid),
        ),
        (pltpu.SemaphoreType.DMA((2,)),),
    )
    base, payload = lax.optimization_barrier((base, payload))
    one = shifted(payload, "row", -1)
    two = shifted(payload, "row", -2)
    notes = (one, two)
    mean, slope, hidden, message = kernel_call(
        functools.partial(forward_kernel, local_confs),
        (
            narrow,
            wide,
            shape((slots, hid), F32),
            shape((rows * columns, 8, slots), F32),
        ),
        [],
        "forward",
        6 * product,
        (near_a, near_b, far_a, far_b, neigh_w, out_w, high, low, base, summed, inverse, stub),
    )
    message, notes = lax.optimization_barrier((message, notes))
    received = lax.all_to_all(message, ("row", "col"), 0, 0, tiled=True)
    received, notes = lax.optimization_barrier((received, notes))
    if columns == 2:
        received, notes = lax.optimization_barrier((received, notes))
        both = jnp.concatenate(notes, axis=0)
        swapped = exchanged(both, "col", 1)
        notes = ((notes[0], swapped[:share]), (notes[1], swapped[share:]))
    else:
        notes = tuple((note, note) for note in notes)
    main = 2 * hid
    grads, loss, d_pre, d_row = kernel_call(
        functools.partial(gradient_kernel, local_confs),
        (
            shape((main + 8, hid), F32),
            shape((1, 1), F32),
            narrow,
            shape((8, slots), F32),
        ),
        [],
        "gradient",
        3 * product,
        (received, chosen, mask, expand, own, mean, slope, hidden),
    )
    scale = math.sqrt(nodes * rows / SEGS)
    (node_total,) = kernel_call(
        functools.partial(own_kernel, local_confs),
        (wide,),
        [],
        "own",
        4 * product,
        (d_pre, self_w, neigh_w, inverse, high, low),
    )

    def later(distance, d_row, node_total, out, factor):
        (result,) = kernel_call(
            functools.partial(later_kernel, local_confs, distance, factor),
            (out,),
            [],
            f"later{distance}",
            10 * product,
            (
                d_row,
                node_total,
                own,
                near_a,
                near_b,
                far_a,
                far_b,
                *notes[distance - 1],
                expand,
                self_w,
                neigh_w,
                out_w,
                bias_w,
            ),
        )
        return result

    total = grads
    for step in range(columns.bit_length() - 1):
        total = total + exchanged(total, "col", 1 << step)
    total, d_row, node_total = lax.optimization_barrier((total, d_row, node_total))
    node_total = later(1, d_row, node_total, wide, 1.0)
    stages = list(row_stages(rows))
    for index, stage in enumerate(stages):
        packet = packed(total, main)
        parts = [packet] + [exchanged(packet, "row", bits) for bits in stage]
        if index == len(stages) - 1:
            break
        total = [unpacked(part, main) for part in parts]
        total = four_summed(total) if len(total) == 4 else total[0] + total[1]
        if index == len(stages) - 2:
            total, d_row, node_total = lax.optimization_barrier((total, d_row, node_total))
    grad_self, grad_neigh, grad_bias, grad_out = finished(parts, main, hid)
    node_grad = later(2, d_row, node_total, narrow, scale)
    return (
        loss.reshape(1),
        grad_self,
        grad_neigh,
        grad_bias.reshape(hid),
        grad_out.reshape(hid),
        node_grad,
    )


def solution(mesh):
    in_specs = (
        P(("groups", "row"), "col"),
        P(("groups", "row"), None, None, None),
        P(("groups", "row"), None),
        P(("groups", "row")),
        P(("groups", "row")),
        P("groups", None),
        P(),
        P(),
        P(),
        P(),
    )
    out_specs = (
        P("groups"),
        P("groups", None),
        P("groups", None),
        P("groups"),
        P("groups"),
        P(("groups", "row"), "col"),
    )
    return jax.shard_map(body, mesh=mesh, in_specs=in_specs, out_specs=out_specs, check_vma=False)
```

```python
import functools
import math

import jax
import jax.numpy as jnp
from jax import lax
from jax.experimental import pallas as pl
from jax.experimental.pallas import tpu as pltpu
from jax.sharding import PartitionSpec as P

REACH = 2
SEGS = 8
WINDOW = REACH + 1
F32 = jnp.float32
BF16 = jnp.bfloat16
HIGHEST = lax.Precision.HIGHEST
VMEM = pl.BlockSpec(memory_space=pltpu.VMEM)
SMEM = pl.BlockSpec(memory_space=pltpu.SMEM)
LIMIT = 24 << 20


def paired(value, steps, phase):
    rows, groups = lax.axis_size("row"), lax.axis_size("groups")
    route = []
    for group in range(groups):
        for row in range(rows):
            target = row + steps if row // steps % 2 == phase else row - steps
            other = group
            if not 0 <= target < rows:
                target = row
                other = group ^ 1 if groups % 2 == 0 else group
            route.append((group * rows + row, other * rows + target))
    return lax.ppermute(value, ("groups", "row"), route)


def shifted(value, axis, steps):
    count = lax.axis_size(axis)
    initial, last = (max(0, -steps), min(count, count - steps))
    return lax.ppermute(value, axis, [(source, source + steps) for source in range(initial, last)])


def around(value):
    order = ((2, 0), (2, 1), (1, 1), (1, 0))
    found = {where: paired(value, *where) for where in order}
    return tuple(found[steps, phase] for steps in (1, 2) for phase in (0, 1))


def panels(steps, first, second):
    even = lax.axis_index("row") // steps % 2 == 0
    return jnp.where(even, second, first), jnp.where(even, first, second)


def exchanged(value, axis, bit):
    count = lax.axis_size(axis)
    return lax.ppermute(value, axis, [(source, source ^ bit) for source in range(count)])


def mm(left, right, contract=((1,), (0,))):
    return lax.dot_general(left, right, (contract, ((), ())), preferred_element_type=F32)


def mm_exact(left, right, contract):
    return lax.dot_general(
        left, right, (contract, ((), ())), precision=HIGHEST, preferred_element_type=F32
    )


def split_two(value):
    high = value.astype(BF16)
    return high, (value - high.astype(F32)).astype(BF16)


def split_three(value):
    high, rest = value.astype(BF16), value
    rest = rest - high.astype(F32)
    middle = rest.astype(BF16)
    return high, middle, (rest - middle.astype(F32)).astype(BF16)


def sigmoid(value):
    return 0.5 + 0.5 * jnp.tanh(0.5 * value)


def iota(dims, dim):
    return lax.broadcasted_iota(jnp.int32, dims, dim)


def column_of(row, count):
    return jnp.broadcast_to(row.astype(F32), (count, row.shape[1])).T


def parcel_kernel(
    local_confs,
    pattern_ref,
    features_ref,
    tiles_ref,
    degree_ref,
    segments_ref,
    pairs_ref,
    bias_ref,
    w_out_ref,
    own_ref,
    high_ref,
    low_ref,
    payload_ref,
    degree_copy_ref,
    segments_copy_ref,
    pairs_copy_ref,
    bias_copy_ref,
    w_out_copy_ref,
    full_ref,
    tiles_buffer,
    sems,
):
    copies = [
        pltpu.make_async_copy(source, target, sems.at[i])
        for i, (source, target) in enumerate(((tiles_ref, tiles_buffer), (features_ref, own_ref)))
    ]
    for copy in copies:
        copy.start()
    degree_copy_ref[...] = degree_ref[...]
    segments_copy_ref[...] = segments_ref[...]
    pairs_copy_ref[...] = pairs_ref[...]
    bias_copy_ref[...] = bias_ref[...]
    w_out_copy_ref[...] = w_out_ref[...]
    nodes = own_ref.shape[0]
    lowest = lax.axis_index("row") - REACH
    step = nodes // local_confs
    segment_row = segments_ref[...]
    notes = jnp.where(iota((8, nodes), 0) == 0, segment_row, degree_ref[...])
    notes = notes.astype(F32).astype(BF16)
    full_ref[WINDOW * step :] = jnp.concatenate([notes] * local_confs, axis=1)
    copies[0].wait()
    for reach in range(WINDOW):
        total = None
        for index in range(tiles_buffer.shape[1]):
            keep = (pattern_ref[0, index] - lowest == reach).astype(F32)
            term = tiles_buffer[0, index].astype(F32) * keep
            total = term if total is None else total + term
        high, low = split_two(total)
        high_ref[reach] = high
        low_ref[reach] = low
        rows = slice(reach * step, (reach + 1) * step)
        for part in range(local_confs):
            full_ref[rows, part * nodes : (part + 1) * nodes] = high[
                part * step : (part + 1) * step
            ]
    share = payload_ref.shape[0]
    start = lax.axis_index("col") * (full_ref.shape[0] - share)
    payload_ref[...] = full_ref[pl.ds(pl.multiple_of(start, 8), share), :]
    copies[1].wait()


def prepare_kernel(
    local_confs,
    self_w_ref,
    neigh_w_ref,
    own_ref,
    high_ref,
    low_ref,
    degree_ref,
    segments_ref,
    pairs_ref,
    bias_ref,
    w_out_ref,
    self_ref,
    neigh_ref,
    out_ref,
    bias_out_ref,
    base_ref,
    summed_ref,
    inverse_ref,
    expand_ref,
    mask_ref,
    chosen_ref,
    stub_ref,
    sems,
):
    copies = [
        pltpu.make_async_copy(source, target, sems.at[i])
        for i, (source, target) in enumerate(((self_w_ref, self_ref), (neigh_w_ref, neigh_ref)))
    ]
    for copy in copies:
        copy.start()
    nodes, hid = own_ref.shape[0], self_ref.shape[0]
    first_conf = lax.axis_index("col") * local_confs
    out_ref[...] = w_out_ref[...]
    bias_out_ref[...] = bias_ref[...]
    inverse_ref[...] = 1.0 / column_of(degree_ref[...], nodes)
    slots = expand_ref.shape[0]
    for conf in range(local_confs):
        cols = slice(conf * hid, (conf + 1) * hid)
        chosen = iota((slots, hid), 0) // SEGS == first_conf + conf
        expand_ref[:, cols] = chosen.astype(F32).astype(BF16)
    segment_row = segments_ref[...]
    segment = column_of(segment_row, slots).astype(jnp.int32)
    mask = (segment == iota((nodes, slots), 1) % SEGS).astype(F32)
    mask_ref[...] = mask
    slot = iota((slots, pairs_ref.shape[1]), 0)
    segment = pairs_ref[0:1, :]
    first = (pairs_ref[1:2, :] * SEGS + segment == slot).astype(F32)
    second = (pairs_ref[2:3, :] * SEGS + segment == slot).astype(F32)
    chosen_ref[...] = (first - second).astype(BF16)
    counts = jnp.sum(mask, axis=0, keepdims=True) * (first_conf == 0).astype(F32)
    sub = iota((8, slots), 0)
    stub_ref[...] = jnp.where(sub == 1, counts, 0.0) + jnp.where(
        sub == 2, segment_row.astype(F32), 0.0
    )
    own = own_ref[...]
    summed_ref[...] = mm(high_ref[REACH], own) + mm(low_ref[REACH], own)
    copies[0].wait()
    for conf in range(local_confs):
        cols = slice(conf * hid, (conf + 1) * hid)
        base_ref[:, cols] = mm(own_ref[:, cols], self_ref[...]) + bias_ref[...]
    copies[1].wait()


def forward_kernel(
    local_confs,
    near_a_ref,
    near_b_ref,
    far_a_ref,
    far_b_ref,
    neigh_ref,
    out_ref,
    high_ref,
    low_ref,
    base_ref,
    summed_ref,
    inverse_ref,
    stub_ref,
    mean_ref,
    slope_ref,
    hidden_ref,
    message_ref,
):
    nodes, hid = base_ref.shape[0], neigh_ref.shape[0]
    summed = summed_ref[...]
    far = panels(2, far_a_ref[...], far_b_ref[...])[0]
    near = panels(1, near_a_ref[...], near_b_ref[...])[0]
    weights = [ref[reach] for reach in (0, 1) for ref in (high_ref, low_ref)]
    summed = summed + mm(
        jnp.concatenate(weights, axis=1), jnp.concatenate([far, far, near, near], axis=0)
    )
    inverse = inverse_ref[...]
    w_out = out_ref[...]
    segment_row = stub_ref[2:3, :].astype(jnp.int32)
    member = (segment_row == iota((SEGS, nodes), 0)).astype(F32).astype(BF16)
    first_conf = lax.axis_index("col") * local_confs
    member = jnp.concatenate([member, member], axis=1)
    hidden_ref[...] = jnp.zeros_like(hidden_ref)
    for conf in range(local_confs):
        cols = slice(conf * hid, (conf + 1) * hid)
        mean = (summed[:, cols] * inverse).astype(BF16)
        mean_ref[:, cols] = mean
        pre = base_ref[:, cols] + mm(mean, neigh_ref[...])
        sigm = sigmoid(pre)
        hidden = pre * sigm
        slope = w_out * (sigm * (1.0 + pre * (1.0 - sigm)))
        slope_ref[:, cols] = slope
        pair = jnp.concatenate(split_two(hidden), axis=0)
        start = pl.multiple_of((first_conf + conf) * SEGS, SEGS)
        hidden_ref[pl.ds(start, SEGS), :] = mm(member, pair)
    scores = mm_exact(jnp.broadcast_to(w_out, (8, hid)), hidden_ref[...], ((1,), (1,)))
    message = jnp.concatenate([scores[0:1], stub_ref[1:2, :]], axis=0)
    for peer in range(message_ref.shape[0]):
        message_ref[peer] = message


def gradient_kernel(
    local_confs,
    received_ref,
    chosen_ref,
    mask_ref,
    expand_ref,
    own_ref,
    mean_ref,
    slope_ref,
    hidden_ref,
    grads_ref,
    loss_ref,
    d_pre_ref,
    d_row_ref,
):
    hid = grads_ref.shape[1]
    total = jnp.sum(received_ref[...], axis=0)
    root = jnp.sqrt(total[1:2])
    scores = total[0:1] / root
    chosen = chosen_ref[...]

    def one_row(row, contract):
        parts = jnp.concatenate([part.astype(F32) for part in split_three(row)], axis=0)
        parts = jnp.concatenate([parts, jnp.zeros((5, row.shape[1]), F32)], axis=0).astype(BF16)
        return jnp.sum(mm(parts, chosen, contract), axis=0, keepdims=True)

    margin = jnp.maximum(0.0, 1.0 - one_row(scores, ((1,), (0,))))
    loss_ref[...] = jnp.sum(margin * margin, axis=1, keepdims=True)
    d_row = one_row(-2.0 * margin, ((1,), (1,))) / root
    d_rows = jnp.broadcast_to(d_row, d_row_ref.shape)
    d_row_ref[...] = d_rows
    factors = split_three(mask_ref[...] * d_row)
    grads = None
    d_bias = None
    for conf in range(local_confs):
        cols = slice(conf * hid, (conf + 1) * hid)
        expand = expand_ref[:, cols]
        d_node = mm(factors[0], expand) + mm(factors[1], expand) + mm(factors[2], expand)
        d_pre = d_node * slope_ref[:, cols]
        d_pre_b = d_pre.astype(BF16)
        d_pre_ref[:, cols] = d_pre_b
        rows = jnp.concatenate([own_ref[:, cols], mean_ref[:, cols]], axis=1)
        term = mm(rows, d_pre_b, ((0,), (0,)))
        grads = term if grads is None else grads + term
        d_bias = d_pre if d_bias is None else d_bias + d_pre
    grads_ref[: 2 * hid] = grads
    d_out = mm_exact(d_rows, hidden_ref[...], ((1,), (0,)))
    d_bias = jnp.sum(d_bias, axis=0, keepdims=True)
    sub = iota((8, hid), 0)
    grads_ref[2 * hid :] = jnp.where(sub == 0, d_bias, 0.0) + jnp.where(sub == 1, d_out, 0.0)


def own_kernel(
    local_confs,
    d_pre_ref,
    self_ref,
    neigh_ref,
    inverse_ref,
    high_ref,
    low_ref,
    total_ref,
):
    hid = self_ref.shape[0]
    inverse = inverse_ref[...]
    for conf in range(local_confs):
        cols = slice(conf * hid, (conf + 1) * hid)
        d_pre = d_pre_ref[:, cols]
        back = (mm(d_pre, neigh_ref[...], ((1,), (1,))) * inverse).astype(BF16)
        total = mm(d_pre, self_ref[...], ((1,), (1,)))
        total = total + mm(high_ref[REACH], back, ((0,), (0,)))
        total_ref[:, cols] = total + mm(low_ref[REACH], back, ((0,), (0,)))


def later_kernel(
    local_confs,
    distance,
    scale,
    d_row_ref,
    total_ref,
    own_ref,
    near_a_ref,
    near_b_ref,
    far_a_ref,
    far_b_ref,
    note_ref,
    note_other_ref,
    expand_ref,
    self_ref,
    neigh_ref,
    out_ref,
    bias_ref,
    result_ref,
):
    hid = self_ref.shape[0]
    nodes = total_ref.shape[0]
    slots = expand_ref.shape[0]
    step = nodes // local_confs
    first_core = lax.axis_index("col") == 0
    upper = jnp.where(first_core, note_ref[...], note_other_ref[...])
    lower = jnp.where(first_core, note_other_ref[...], note_ref[...])
    share = upper.shape[0]
    note = jnp.concatenate([upper, lower[2 * share - WINDOW * step - 8 :]], axis=0)
    notes = note[WINDOW * step :, :nodes].astype(F32)
    segment = column_of(notes[0:1], slots).astype(jnp.int32)
    inverse = 1.0 / jnp.maximum(column_of(notes[1:2], nodes), 1.0)
    present = lax.axis_index("row") + distance < lax.axis_size("row")
    mask = (segment == iota((nodes, slots), 1) % SEGS).astype(F32) * present.astype(F32)
    factors = split_two(mask * d_row_ref[0:1, :])
    tiles = []
    for reach in range(WINDOW):
        rows = slice(reach * step, (reach + 1) * step)
        parts = [note[rows, part * nodes : (part + 1) * nodes] for part in range(local_confs)]
        tiles.append(jnp.concatenate(parts, axis=0))
    weights = jnp.concatenate([self_ref[...], neigh_ref[...]], axis=0)
    w_out = out_ref[...]
    before, after = panels(1, near_a_ref[...], near_b_ref[...])
    sources = [before, own_ref[...], after]
    if distance == 2:
        sources = sources[1:] + [panels(2, far_a_ref[...], far_b_ref[...])[1]]
    summed = mm(jnp.concatenate(tiles, axis=1), jnp.concatenate(sources, axis=0))
    for conf in range(local_confs):
        cols = slice(conf * hid, (conf + 1) * hid)
        mean = (summed[:, cols] * inverse).astype(BF16)
        pre = mm(jnp.concatenate([sources[2][:, cols], mean], axis=1), weights) + bias_ref[...]
        sigm = sigmoid(pre)
        slope = w_out * (sigm * (1.0 + pre * (1.0 - sigm)))
        expand = expand_ref[:, cols]
        d_node = mm(factors[0], expand) + mm(factors[1], expand)
        d_pre = (d_node * slope).astype(BF16)
        back = (mm(d_pre, neigh_ref[...], ((1,), (1,))) * inverse).astype(BF16)
        total = total_ref[:, cols] + mm(tiles[REACH - distance], back, ((0,), (0,)))
        result_ref[:, cols] = (total * scale).astype(result_ref.dtype)


def final_kernel(main, count, *refs):
    hid = refs[0].shape[1]
    parts = [ref[...].astype(F32) for ref in refs[:count]]
    if count == 4:
        total = (parts[0] + parts[1]) + (parts[2] + parts[3])
    else:
        total = parts[0] + parts[1]
    self_ref, neigh_ref, bias_ref, out_ref = refs[count:]
    self_ref[...] = total[:hid]
    neigh_ref[...] = total[hid:main]
    extra = (total.shape[0] - main) // 3
    rows = [vectors(part, main, extra) for part in parts]
    if count == 4:
        row = (rows[0] + rows[1]) + (rows[2] + rows[3])
    else:
        row = rows[0] + rows[1]
    bias_ref[...] = row[0:1]
    out_ref[...] = row[1:2]


def vectors(message, main, extra):
    high, middle, last = (
        message[main + i * extra : main + (i + 1) * extra] for i in range(3)
    )
    return high + middle + last


def rounded(value):
    return lax.reduce_precision(value, 8, 7)


def packed(total, main):
    vectors = total[main:]
    high = rounded(vectors)
    middle = rounded(vectors - high)
    last = rounded(vectors - high - middle)
    return jnp.concatenate([rounded(total[:main]), high, middle, last], axis=0).astype(BF16)


def unpacked(message, main):
    message = message.astype(F32)
    extra = (message.shape[0] - main) // 3
    parts = [message[main + i * extra : main + (i + 1) * extra] for i in range(3)]
    return jnp.concatenate([message[:main], parts[0] + parts[1] + parts[2]], axis=0)


def row_stages(count):
    stride = 1
    while stride < count:
        yield [stride * k for k in (1, 2, 3) if stride * k < count]
        stride *= 4


def finished(parts, main, hid):
    outs = (shape((hid, hid), F32), shape((hid, hid), F32), shape((1, hid), F32), shape((1, hid), F32))
    return kernel_call(
        functools.partial(final_kernel, main, len(parts)), outs, [], "finish", 1 << 20, parts
    )


def four_summed(parts):
    return (parts[0] + parts[1]) + (parts[2] + parts[3])


def shape(dims, dtype):
    return jax.ShapeDtypeStruct(dims, dtype)


def kernel_call(kernel, outs, spaces, name, flops, operands, scratch=()):
    moved = sum(math.prod(leaf.shape) * leaf.dtype.itemsize for leaf in tuple(operands) + tuple(outs))
    spaces = list(spaces) + [pltpu.VMEM] * (len(operands) - len(spaces))
    return pl.pallas_call(
        kernel,
        out_shape=outs,
        in_specs=[pl.BlockSpec(memory_space=space) for space in spaces],
        out_specs=(pl.BlockSpec(memory_space=pltpu.VMEM),) * len(outs),
        scratch_shapes=scratch,
        compiler_params=pltpu.CompilerParams(vmem_limit_bytes=LIMIT),
        cost_estimate=pl.CostEstimate(flops=flops, bytes_accessed=moved, transcendentals=0),
        name=name,
    )(*operands)


def body(features, tiles, pattern, degrees, segments, pairs, w_self, w_neigh, bias, w_out):
    nodes, width = features.shape
    hid = w_self.shape[0]
    local_confs = width // hid
    rows, columns = lax.axis_size("row"), lax.axis_size("col")
    product = 2 * nodes * nodes * width
    slots = local_confs * columns * SEGS
    near_a, near_b, far_a, far_b = around(features)
    wide = shape((nodes, width), F32)
    narrow = shape((nodes, width), BF16)
    square = shape((nodes, nodes), F32)
    weight = shape((hid, hid), BF16)
    tile_set = shape((WINDOW, nodes, nodes), BF16)
    in_hbm = [
        pltpu.with_memory_space_constraint(value, pltpu.HBM)
        for value in (features, tiles, w_self, w_neigh)
    ]
    note_rows = WINDOW * (nodes // local_confs) + 8
    share = -(-note_rows // 16) * 8 if columns == 2 else note_rows
    own, high, low, payload, degree_row, segment_row, pair_rows, bias_row, out_row = kernel_call(
        functools.partial(parcel_kernel, local_confs),
        (
            narrow,
            tile_set,
            tile_set,
            shape((share, width), BF16),
            shape((1, nodes), jnp.int32),
            shape((1, nodes), jnp.int32),
            shape((3, pairs.shape[0]), jnp.int32),
            shape((1, hid), F32),
            shape((1, hid), F32),
        ),
        [pltpu.SMEM] + [pltpu.HBM] * 2,
        "parcel",
        product,
        (
            pattern,
            in_hbm[0],
            in_hbm[1],
            degrees.reshape(1, nodes),
            segments.reshape(1, nodes),
            pairs.T,
            bias.reshape(1, hid),
            w_out.reshape(1, hid),
        ),
        (
            pltpu.VMEM((note_rows, width), BF16),
            pltpu.VMEM(tiles.shape, tiles.dtype),
            pltpu.SemaphoreType.DMA((2,)),
        ),
    )
    (
        self_w,
        neigh_w,
        out_w,
        bias_w,
        base,
        summed,
        inverse,
        expand,
        mask,
        chosen,
        stub,
    ) = kernel_call(
        functools.partial(prepare_kernel, local_confs),
        (
            weight,
            weight,
            shape((1, hid), F32),
            shape((1, hid), F32),
            wide,
            wide,
            square,
            shape((slots, width), BF16),
            shape((nodes, slots), F32),
            shape((slots, pairs.shape[0]), BF16),
            shape((8, slots), F32),
        ),
        [pltpu.HBM] * 2,
        "prepare",
        3 * product,
        (
            in_hbm[2],
            in_hbm[3],
            own,
            high,
            low,
            degree_row,
            segment_row,
            pair_rows,
            bias_row,
            out_row,
        ),
        (pltpu.SemaphoreType.DMA((2,)),),
    )
    base, payload = lax.optimization_barrier((base, payload))
    one = shifted(payload, "row", -1)
    two = shifted(payload, "row", -2)
    notes = (one, two)
    mean, slope, hidden, message = kernel_call(
        functools.partial(forward_kernel, local_confs),
        (
            narrow,
            wide,
            shape((slots, hid), F32),
            shape((rows * columns, 2, slots), F32),
        ),
        [],
        "forward",
        6 * product,
        (near_a, near_b, far_a, far_b, neigh_w, out_w, high, low, base, summed, inverse, stub),
    )
    message, notes = lax.optimization_barrier((message, notes))
    received = lax.all_to_all(message, ("row", "col"), 0, 0, tiled=True)
    received, notes = lax.optimization_barrier((received, notes))
    if columns == 2:
        received, notes = lax.optimization_barrier((received, notes))
        both = jnp.concatenate(notes, axis=0)
        swapped = exchanged(both, "col", 1)
        notes = ((notes[0], swapped[:share]), (notes[1], swapped[share:]))
    else:
        notes = tuple((note, note) for note in notes)
    main = 2 * hid
    grads, loss, d_pre, d_row = kernel_call(
        functools.partial(gradient_kernel, local_confs),
        (
            shape((main + 8, hid), F32),
            shape((1, 1), F32),
            narrow,
            shape((8, slots), F32),
        ),
        [],
        "gradient",
        3 * product,
        (received, chosen, mask, expand, own, mean, slope, hidden),
    )
    scale = math.sqrt(nodes * rows / SEGS)
    (node_total,) = kernel_call(
        functools.partial(own_kernel, local_confs),
        (wide,),
        [],
        "own",
        4 * product,
        (d_pre, self_w, neigh_w, inverse, high, low),
    )

    def later(distance, d_row, node_total, out, factor):
        (result,) = kernel_call(
            functools.partial(later_kernel, local_confs, distance, factor),
            (out,),
            [],
            f"later{distance}",
            10 * product,
            (
                d_row,
                node_total,
                own,
                near_a,
                near_b,
                far_a,
                far_b,
                *notes[distance - 1],
                expand,
                self_w,
                neigh_w,
                out_w,
                bias_w,
            ),
        )
        return result

    total = grads
    for step in range(columns.bit_length() - 1):
        total = total + exchanged(total, "col", 1 << step)
    total, d_row, node_total = lax.optimization_barrier((total, d_row, node_total))
    node_total = later(1, d_row, node_total, wide, 1.0)
    stages = list(row_stages(rows))
    for index, stage in enumerate(stages):
        packet = packed(total, main)
        parts = [packet] + [exchanged(packet, "row", bits) for bits in stage]
        if index == len(stages) - 1:
            break
        total = [unpacked(part, main) for part in parts]
        total = four_summed(total) if len(total) == 4 else total[0] + total[1]
        if index == len(stages) - 2:
            total, d_row, node_total = lax.optimization_barrier((total, d_row, node_total))
    grad_self, grad_neigh, grad_bias, grad_out = finished(parts, main, hid)
    node_grad = later(2, d_row, node_total, narrow, scale)
    return (
        loss.reshape(1),
        grad_self,
        grad_neigh,
        grad_bias.reshape(hid),
        grad_out.reshape(hid),
        node_grad,
    )


def solution(mesh):
    in_specs = (
        P(("groups", "row"), "col"),
        P(("groups", "row"), None, None, None),
        P(("groups", "row"), None),
        P(("groups", "row")),
        P(("groups", "row")),
        P("groups", None),
        P(),
        P(),
        P(),
        P(),
    )
    out_specs = (
        P("groups"),
        P("groups", None),
        P("groups", None),
        P("groups"),
        P("groups"),
        P(("groups", "row"), "col"),
    )
    return jax.shard_map(body, mesh=mesh, in_specs=in_specs, out_specs=out_specs, check_vma=False)
```

```python
import functools
import math

import jax
import jax.numpy as jnp
from jax import lax
from jax.experimental import pallas as pl
from jax.experimental.pallas import tpu as pltpu
from jax.sharding import PartitionSpec as P

REACH = 2
SEGS = 8
WINDOW = REACH + 1
F32 = jnp.float32
BF16 = jnp.bfloat16
HIGHEST = lax.Precision.HIGHEST
VMEM = pl.BlockSpec(memory_space=pltpu.VMEM)
SMEM = pl.BlockSpec(memory_space=pltpu.SMEM)
LIMIT = 24 << 20


def paired(value, steps, phase):
    rows, groups = lax.axis_size("row"), lax.axis_size("groups")
    route = []
    for group in range(groups):
        for row in range(rows):
            target = row + steps if row // steps % 2 == phase else row - steps
            other = group
            if not 0 <= target < rows:
                target = row
                other = group ^ 1 if groups % 2 == 0 else group
            route.append((group * rows + row, other * rows + target))
    return lax.ppermute(value, ("groups", "row"), route)


def shifted(value, axis, steps):
    count = lax.axis_size(axis)
    initial, last = (max(0, -steps), min(count, count - steps))
    return lax.ppermute(value, axis, [(source, source + steps) for source in range(initial, last)])


def around(value):
    order = ((2, 0), (2, 1), (1, 1), (1, 0))
    found = {where: paired(value, *where) for where in order}
    return tuple(found[steps, phase] for steps in (1, 2) for phase in (0, 1))


def panels(steps, first, second):
    even = lax.axis_index("row") // steps % 2 == 0
    return jnp.where(even, second, first), jnp.where(even, first, second)


def exchanged(value, axis, bit):
    count = lax.axis_size(axis)
    return lax.ppermute(value, axis, [(source, source ^ bit) for source in range(count)])


def mm(left, right, contract=((1,), (0,))):
    return lax.dot_general(left, right, (contract, ((), ())), preferred_element_type=F32)


def mm_exact(left, right, contract):
    return lax.dot_general(
        left, right, (contract, ((), ())), precision=HIGHEST, preferred_element_type=F32
    )


def split_two(value):
    high = value.astype(BF16)
    return high, (value - high.astype(F32)).astype(BF16)


def split_three(value):
    high, rest = value.astype(BF16), value
    rest = rest - high.astype(F32)
    middle = rest.astype(BF16)
    return high, middle, (rest - middle.astype(F32)).astype(BF16)


def sigmoid(value):
    return 0.5 + 0.5 * jnp.tanh(0.5 * value)


def iota(dims, dim):
    return lax.broadcasted_iota(jnp.int32, dims, dim)


def column_of(row, count):
    return jnp.broadcast_to(row.astype(F32), (count, row.shape[1])).T


def parcel_kernel(
    local_confs,
    pattern_ref,
    features_ref,
    tiles_ref,
    degree_ref,
    segments_ref,
    pairs_ref,
    bias_ref,
    w_out_ref,
    own_ref,
    high_ref,
    low_ref,
    payload_ref,
    degree_copy_ref,
    segments_copy_ref,
    pairs_copy_ref,
    bias_copy_ref,
    w_out_copy_ref,
    full_ref,
    tiles_buffer,
    sems,
):
    copies = [
        pltpu.make_async_copy(source, target, sems.at[i])
        for i, (source, target) in enumerate(((tiles_ref, tiles_buffer), (features_ref, own_ref)))
    ]
    for copy in copies:
        copy.start()
    degree_copy_ref[...] = degree_ref[...]
    segments_copy_ref[...] = segments_ref[...]
    pairs_copy_ref[...] = pairs_ref[...]
    bias_copy_ref[...] = bias_ref[...]
    w_out_copy_ref[...] = w_out_ref[...]
    nodes = own_ref.shape[0]
    lowest = lax.axis_index("row") - REACH
    step = nodes // local_confs
    segment_row = segments_ref[...]
    notes = jnp.where(iota((8, nodes), 0) == 0, segment_row, degree_ref[...])
    notes = notes.astype(F32).astype(BF16)
    full_ref[WINDOW * step :] = jnp.concatenate([notes] * local_confs, axis=1)
    copies[0].wait()
    for reach in range(WINDOW):
        total = None
        for index in range(tiles_buffer.shape[1]):
            keep = (pattern_ref[0, index] - lowest == reach).astype(F32)
            term = tiles_buffer[0, index].astype(F32) * keep
            total = term if total is None else total + term
        high, low = split_two(total)
        high_ref[reach] = high
        low_ref[reach] = low
        rows = slice(reach * step, (reach + 1) * step)
        for part in range(local_confs):
            full_ref[rows, part * nodes : (part + 1) * nodes] = high[
                part * step : (part + 1) * step
            ]
    share = payload_ref.shape[0]
    start = lax.axis_index("col") * (full_ref.shape[0] - share)
    payload_ref[...] = full_ref[pl.ds(pl.multiple_of(start, 8), share), :]
    copies[1].wait()


def prepare_kernel(
    local_confs,
    self_w_ref,
    neigh_w_ref,
    own_ref,
    high_ref,
    low_ref,
    degree_ref,
    segments_ref,
    pairs_ref,
    bias_ref,
    w_out_ref,
    self_ref,
    neigh_ref,
    out_ref,
    bias_out_ref,
    base_ref,
    summed_ref,
    inverse_ref,
    expand_ref,
    mask_ref,
    chosen_ref,
    stub_ref,
    sems,
):
    copies = [
        pltpu.make_async_copy(source, target, sems.at[i])
        for i, (source, target) in enumerate(((self_w_ref, self_ref), (neigh_w_ref, neigh_ref)))
    ]
    for copy in copies:
        copy.start()
    nodes, hid = own_ref.shape[0], self_ref.shape[0]
    first_conf = lax.axis_index("col") * local_confs
    out_ref[...] = w_out_ref[...]
    bias_out_ref[...] = bias_ref[...]
    inverse_ref[...] = 1.0 / column_of(degree_ref[...], nodes)
    slots = expand_ref.shape[0]
    for conf in range(local_confs):
        cols = slice(conf * hid, (conf + 1) * hid)
        chosen = iota((slots, hid), 0) // SEGS == first_conf + conf
        expand_ref[:, cols] = chosen.astype(F32).astype(BF16)
    segment_row = segments_ref[...]
    segment = column_of(segment_row, slots).astype(jnp.int32)
    mask = (segment == iota((nodes, slots), 1) % SEGS).astype(F32)
    mask_ref[...] = mask
    slot = iota((slots, pairs_ref.shape[1]), 0)
    segment = pairs_ref[0:1, :]
    first = (pairs_ref[1:2, :] * SEGS + segment == slot).astype(F32)
    second = (pairs_ref[2:3, :] * SEGS + segment == slot).astype(F32)
    chosen_ref[...] = (first - second).astype(BF16)
    counts = jnp.sum(mask, axis=0, keepdims=True) * (first_conf == 0).astype(F32)
    sub = iota((8, slots), 0)
    stub_ref[...] = jnp.where(sub == 1, counts, 0.0) + jnp.where(
        sub == 2, segment_row.astype(F32), 0.0
    )
    own = own_ref[...]
    summed_ref[...] = mm(high_ref[REACH], own) + mm(low_ref[REACH], own)
    copies[0].wait()
    for conf in range(local_confs):
        cols = slice(conf * hid, (conf + 1) * hid)
        base_ref[:, cols] = mm(own_ref[:, cols], self_ref[...]) + bias_ref[...]
    copies[1].wait()


def forward_kernel(
    local_confs,
    near_a_ref,
    near_b_ref,
    far_a_ref,
    far_b_ref,
    neigh_ref,
    out_ref,
    high_ref,
    low_ref,
    base_ref,
    summed_ref,
    inverse_ref,
    stub_ref,
    mean_ref,
    slope_ref,
    hidden_ref,
    message_ref,
):
    nodes, hid = base_ref.shape[0], neigh_ref.shape[0]
    summed = summed_ref[...]
    far = panels(2, far_a_ref[...], far_b_ref[...])[0]
    near = panels(1, near_a_ref[...], near_b_ref[...])[0]
    weights = [ref[reach] for reach in (0, 1) for ref in (high_ref, low_ref)]
    summed = summed + mm(
        jnp.concatenate(weights, axis=1), jnp.concatenate([far, far, near, near], axis=0)
    )
    inverse = inverse_ref[...]
    w_out = out_ref[...]
    segment_row = stub_ref[2:3, :].astype(jnp.int32)
    member = (segment_row == iota((SEGS, nodes), 0)).astype(F32).astype(BF16)
    first_conf = lax.axis_index("col") * local_confs
    member = jnp.concatenate([member, member], axis=1)
    hidden_ref[...] = jnp.zeros_like(hidden_ref)
    for conf in range(local_confs):
        cols = slice(conf * hid, (conf + 1) * hid)
        mean = (summed[:, cols] * inverse).astype(BF16)
        mean_ref[:, cols] = mean
        pre = base_ref[:, cols] + mm(mean, neigh_ref[...])
        sigm = sigmoid(pre)
        hidden = pre * sigm
        slope = w_out * (sigm * (1.0 + pre * (1.0 - sigm)))
        slope_ref[:, cols] = slope
        pair = jnp.concatenate(split_two(hidden), axis=0)
        start = pl.multiple_of((first_conf + conf) * SEGS, SEGS)
        hidden_ref[pl.ds(start, SEGS), :] = mm(member, pair)
    scores = mm_exact(jnp.broadcast_to(w_out, (8, hid)), hidden_ref[...], ((1,), (1,)))
    message = jnp.concatenate([scores[0:1], stub_ref[1:2, :]], axis=0)
    for peer in range(message_ref.shape[0]):
        message_ref[peer] = message


def gradient_kernel(
    local_confs,
    received_ref,
    chosen_ref,
    mask_ref,
    expand_ref,
    own_ref,
    mean_ref,
    slope_ref,
    hidden_ref,
    grads_ref,
    loss_ref,
    d_pre_ref,
    d_row_ref,
):
    hid = grads_ref.shape[1]
    total = jnp.sum(received_ref[...], axis=0)
    root = jnp.sqrt(total[1:2])
    scores = total[0:1] / root
    chosen = chosen_ref[...]

    def one_row(row, contract):
        parts = jnp.concatenate([part.astype(F32) for part in split_three(row)], axis=0)
        parts = jnp.concatenate([parts, jnp.zeros((5, row.shape[1]), F32)], axis=0).astype(BF16)
        return jnp.sum(mm(parts, chosen, contract), axis=0, keepdims=True)

    margin = jnp.maximum(0.0, 1.0 - one_row(scores, ((1,), (0,))))
    loss_ref[...] = jnp.sum(margin * margin, axis=1, keepdims=True)
    d_row = one_row(-2.0 * margin, ((1,), (1,))) / root
    d_rows = jnp.broadcast_to(d_row, d_row_ref.shape)
    d_row_ref[...] = d_rows
    factors = split_three(mask_ref[...] * d_row)
    expand = expand_ref[...]
    d_node = mm(factors[0], expand) + mm(factors[1], expand) + mm(factors[2], expand)
    grads = None
    d_bias = None
    for conf in range(local_confs):
        cols = slice(conf * hid, (conf + 1) * hid)
        d_pre = d_node[:, cols] * slope_ref[:, cols]
        d_pre_b = d_pre.astype(BF16)
        d_pre_ref[:, cols] = d_pre_b
        rows = jnp.concatenate([own_ref[:, cols], mean_ref[:, cols]], axis=1)
        term = mm(rows, d_pre_b, ((0,), (0,)))
        grads = term if grads is None else grads + term
        d_bias = d_pre if d_bias is None else d_bias + d_pre
    grads_ref[: 2 * hid] = grads
    d_out = mm_exact(d_rows, hidden_ref[...], ((1,), (0,)))
    d_bias = jnp.sum(d_bias, axis=0, keepdims=True)
    sub = iota((8, hid), 0)
    grads_ref[2 * hid :] = jnp.where(sub == 0, d_bias, 0.0) + jnp.where(sub == 1, d_out, 0.0)


def own_kernel(
    local_confs,
    d_pre_ref,
    self_ref,
    neigh_ref,
    inverse_ref,
    high_ref,
    low_ref,
    total_ref,
):
    hid = self_ref.shape[0]
    inverse = inverse_ref[...]
    for conf in range(local_confs):
        cols = slice(conf * hid, (conf + 1) * hid)
        d_pre = d_pre_ref[:, cols]
        back = (mm(d_pre, neigh_ref[...], ((1,), (1,))) * inverse).astype(BF16)
        total = mm(d_pre, self_ref[...], ((1,), (1,)))
        total = total + mm(high_ref[REACH], back, ((0,), (0,)))
        total_ref[:, cols] = total + mm(low_ref[REACH], back, ((0,), (0,)))


def later_kernel(
    local_confs,
    distance,
    scale,
    d_row_ref,
    total_ref,
    own_ref,
    near_a_ref,
    near_b_ref,
    far_a_ref,
    far_b_ref,
    note_ref,
    note_other_ref,
    expand_ref,
    self_ref,
    neigh_ref,
    out_ref,
    bias_ref,
    result_ref,
):
    hid = self_ref.shape[0]
    nodes = total_ref.shape[0]
    slots = expand_ref.shape[0]
    step = nodes // local_confs
    first_core = lax.axis_index("col") == 0
    upper = jnp.where(first_core, note_ref[...], note_other_ref[...])
    lower = jnp.where(first_core, note_other_ref[...], note_ref[...])
    share = upper.shape[0]
    note = jnp.concatenate([upper, lower[2 * share - WINDOW * step - 8 :]], axis=0)
    notes = note[WINDOW * step :, :nodes].astype(F32)
    segment = column_of(notes[0:1], slots).astype(jnp.int32)
    inverse = 1.0 / jnp.maximum(column_of(notes[1:2], nodes), 1.0)
    present = lax.axis_index("row") + distance < lax.axis_size("row")
    mask = (segment == iota((nodes, slots), 1) % SEGS).astype(F32) * present.astype(F32)
    factors = split_two(mask * d_row_ref[0:1, :])
    tiles = []
    for reach in range(WINDOW):
        rows = slice(reach * step, (reach + 1) * step)
        parts = [note[rows, part * nodes : (part + 1) * nodes] for part in range(local_confs)]
        tiles.append(jnp.concatenate(parts, axis=0))
    weights = jnp.concatenate([self_ref[...], neigh_ref[...]], axis=0)
    w_out = out_ref[...]
    before, after = panels(1, near_a_ref[...], near_b_ref[...])
    sources = [before, own_ref[...], after]
    if distance == 2:
        sources = sources[1:] + [panels(2, far_a_ref[...], far_b_ref[...])[1]]
    summed = mm(jnp.concatenate(tiles, axis=1), jnp.concatenate(sources, axis=0))
    for conf in range(local_confs):
        cols = slice(conf * hid, (conf + 1) * hid)
        mean = (summed[:, cols] * inverse).astype(BF16)
        pre = mm(jnp.concatenate([sources[2][:, cols], mean], axis=1), weights) + bias_ref[...]
        sigm = sigmoid(pre)
        slope = w_out * (sigm * (1.0 + pre * (1.0 - sigm)))
        expand = expand_ref[:, cols]
        d_node = mm(factors[0], expand) + mm(factors[1], expand)
        d_pre = (d_node * slope).astype(BF16)
        back = (mm(d_pre, neigh_ref[...], ((1,), (1,))) * inverse).astype(BF16)
        total = total_ref[:, cols] + mm(tiles[REACH - distance], back, ((0,), (0,)))
        result_ref[:, cols] = (total * scale).astype(result_ref.dtype)


def final_kernel(main, count, *refs):
    hid = refs[0].shape[1]
    parts = [ref[...].astype(F32) for ref in refs[:count]]
    if count == 4:
        total = (parts[0] + parts[1]) + (parts[2] + parts[3])
    else:
        total = parts[0] + parts[1]
    self_ref, neigh_ref, bias_ref, out_ref = refs[count:]
    self_ref[...] = total[:hid]
    neigh_ref[...] = total[hid:main]
    extra = (total.shape[0] - main) // 3
    rows = [vectors(part, main, extra) for part in parts]
    if count == 4:
        row = (rows[0] + rows[1]) + (rows[2] + rows[3])
    else:
        row = rows[0] + rows[1]
    bias_ref[...] = row[0:1]
    out_ref[...] = row[1:2]


def vectors(message, main, extra):
    high, middle, last = (
        message[main + i * extra : main + (i + 1) * extra] for i in range(3)
    )
    return high + middle + last


def rounded(value):
    return lax.reduce_precision(value, 8, 7)


def packed(total, main):
    vectors = total[main:]
    high = rounded(vectors)
    middle = rounded(vectors - high)
    last = rounded(vectors - high - middle)
    return jnp.concatenate([rounded(total[:main]), high, middle, last], axis=0).astype(BF16)


def unpacked(message, main):
    message = message.astype(F32)
    extra = (message.shape[0] - main) // 3
    parts = [message[main + i * extra : main + (i + 1) * extra] for i in range(3)]
    return jnp.concatenate([message[:main], parts[0] + parts[1] + parts[2]], axis=0)


def row_stages(count):
    stride = 1
    while stride < count:
        yield [stride * k for k in (1, 2, 3) if stride * k < count]
        stride *= 4


def finished(parts, main, hid):
    outs = (shape((hid, hid), F32), shape((hid, hid), F32), shape((1, hid), F32), shape((1, hid), F32))
    return kernel_call(
        functools.partial(final_kernel, main, len(parts)), outs, [], "finish", 1 << 20, parts
    )


def four_summed(parts):
    return (parts[0] + parts[1]) + (parts[2] + parts[3])


def shape(dims, dtype):
    return jax.ShapeDtypeStruct(dims, dtype)


def kernel_call(kernel, outs, spaces, name, flops, operands, scratch=()):
    moved = sum(math.prod(leaf.shape) * leaf.dtype.itemsize for leaf in tuple(operands) + tuple(outs))
    spaces = list(spaces) + [pltpu.VMEM] * (len(operands) - len(spaces))
    return pl.pallas_call(
        kernel,
        out_shape=outs,
        in_specs=[pl.BlockSpec(memory_space=space) for space in spaces],
        out_specs=(pl.BlockSpec(memory_space=pltpu.VMEM),) * len(outs),
        scratch_shapes=scratch,
        compiler_params=pltpu.CompilerParams(vmem_limit_bytes=LIMIT),
        cost_estimate=pl.CostEstimate(flops=flops, bytes_accessed=moved, transcendentals=0),
        name=name,
    )(*operands)


def body(features, tiles, pattern, degrees, segments, pairs, w_self, w_neigh, bias, w_out):
    nodes, width = features.shape
    hid = w_self.shape[0]
    local_confs = width // hid
    rows, columns = lax.axis_size("row"), lax.axis_size("col")
    product = 2 * nodes * nodes * width
    slots = local_confs * columns * SEGS
    near_a, near_b, far_a, far_b = around(features)
    wide = shape((nodes, width), F32)
    narrow = shape((nodes, width), BF16)
    square = shape((nodes, nodes), F32)
    weight = shape((hid, hid), BF16)
    tile_set = shape((WINDOW, nodes, nodes), BF16)
    in_hbm = [
        pltpu.with_memory_space_constraint(value, pltpu.HBM)
        for value in (features, tiles, w_self, w_neigh)
    ]
    note_rows = WINDOW * (nodes // local_confs) + 8
    share = -(-note_rows // 16) * 8 if columns == 2 else note_rows
    own, high, low, payload, degree_row, segment_row, pair_rows, bias_row, out_row = kernel_call(
        functools.partial(parcel_kernel, local_confs),
        (
            narrow,
            tile_set,
            tile_set,
            shape((share, width), BF16),
            shape((1, nodes), jnp.int32),
            shape((1, nodes), jnp.int32),
            shape((3, pairs.shape[0]), jnp.int32),
            shape((1, hid), F32),
            shape((1, hid), F32),
        ),
        [pltpu.SMEM] + [pltpu.HBM] * 2,
        "parcel",
        product,
        (
            pattern,
            in_hbm[0],
            in_hbm[1],
            degrees.reshape(1, nodes),
            segments.reshape(1, nodes),
            pairs.T,
            bias.reshape(1, hid),
            w_out.reshape(1, hid),
        ),
        (
            pltpu.VMEM((note_rows, width), BF16),
            pltpu.VMEM(tiles.shape, tiles.dtype),
            pltpu.SemaphoreType.DMA((2,)),
        ),
    )
    (
        self_w,
        neigh_w,
        out_w,
        bias_w,
        base,
        summed,
        inverse,
        expand,
        mask,
        chosen,
        stub,
    ) = kernel_call(
        functools.partial(prepare_kernel, local_confs),
        (
            weight,
            weight,
            shape((1, hid), F32),
            shape((1, hid), F32),
            wide,
            wide,
            square,
            shape((slots, width), BF16),
            shape((nodes, slots), F32),
            shape((slots, pairs.shape[0]), BF16),
            shape((8, slots), F32),
        ),
        [pltpu.HBM] * 2,
        "prepare",
        3 * product,
        (
            in_hbm[2],
            in_hbm[3],
            own,
            high,
            low,
            degree_row,
            segment_row,
            pair_rows,
            bias_row,
            out_row,
        ),
        (pltpu.SemaphoreType.DMA((2,)),),
    )
    base, payload = lax.optimization_barrier((base, payload))
    one = shifted(payload, "row", -1)
    two = shifted(payload, "row", -2)
    notes = (one, two)
    mean, slope, hidden, message = kernel_call(
        functools.partial(forward_kernel, local_confs),
        (
            narrow,
            wide,
            shape((slots, hid), F32),
            shape((rows * columns, 2, slots), F32),
        ),
        [],
        "forward",
        6 * product,
        (near_a, near_b, far_a, far_b, neigh_w, out_w, high, low, base, summed, inverse, stub),
    )
    message, notes = lax.optimization_barrier((message, notes))
    received = lax.all_to_all(message, ("row", "col"), 0, 0, tiled=True)
    received, notes = lax.optimization_barrier((received, notes))
    if columns == 2:
        received, notes = lax.optimization_barrier((received, notes))
        both = jnp.concatenate(notes, axis=0)
        swapped = exchanged(both, "col", 1)
        notes = ((notes[0], swapped[:share]), (notes[1], swapped[share:]))
    else:
        notes = tuple((note, note) for note in notes)
    main = 2 * hid
    grads, loss, d_pre, d_row = kernel_call(
        functools.partial(gradient_kernel, local_confs),
        (
            shape((main + 8, hid), F32),
            shape((1, 1), F32),
            narrow,
            shape((8, slots), F32),
        ),
        [],
        "gradient",
        3 * product,
        (received, chosen, mask, expand, own, mean, slope, hidden),
    )
    scale = math.sqrt(nodes * rows / SEGS)
    (node_total,) = kernel_call(
        functools.partial(own_kernel, local_confs),
        (wide,),
        [],
        "own",
        4 * product,
        (d_pre, self_w, neigh_w, inverse, high, low),
    )

    def later(distance, d_row, node_total, out, factor):
        (result,) = kernel_call(
            functools.partial(later_kernel, local_confs, distance, factor),
            (out,),
            [],
            f"later{distance}",
            10 * product,
            (
                d_row,
                node_total,
                own,
                near_a,
                near_b,
                far_a,
                far_b,
                *notes[distance - 1],
                expand,
                self_w,
                neigh_w,
                out_w,
                bias_w,
            ),
        )
        return result

    total = grads
    for step in range(columns.bit_length() - 1):
        total = total + exchanged(total, "col", 1 << step)
    total, d_row, node_total = lax.optimization_barrier((total, d_row, node_total))
    node_total = later(1, d_row, node_total, wide, 1.0)
    stages = list(row_stages(rows))
    for index, stage in enumerate(stages):
        packet = packed(total, main)
        parts = [packet] + [exchanged(packet, "row", bits) for bits in stage]
        if index == len(stages) - 1:
            break
        total = [unpacked(part, main) for part in parts]
        total = four_summed(total) if len(total) == 4 else total[0] + total[1]
        if index == len(stages) - 2:
            total, d_row, node_total = lax.optimization_barrier((total, d_row, node_total))
    grad_self, grad_neigh, grad_bias, grad_out = finished(parts, main, hid)
    node_grad = later(2, d_row, node_total, narrow, scale)
    return (
        loss.reshape(1),
        grad_self,
        grad_neigh,
        grad_bias.reshape(hid),
        grad_out.reshape(hid),
        node_grad,
    )


def solution(mesh):
    in_specs = (
        P(("groups", "row"), "col"),
        P(("groups", "row"), None, None, None),
        P(("groups", "row"), None),
        P(("groups", "row")),
        P(("groups", "row")),
        P("groups", None),
        P(),
        P(),
        P(),
        P(),
    )
    out_specs = (
        P("groups"),
        P("groups", None),
        P("groups", None),
        P("groups"),
        P("groups"),
        P(("groups", "row"), "col"),
    )
    return jax.shard_map(body, mesh=mesh, in_specs=in_specs, out_specs=out_specs, check_vma=False)
```
